32 devices in a mesh: grp: 2 (over y), slab: 16 (over z, x, core).
Axes of the slice: x: 2, y: 2, z: 4, core: 2. Of those that a mesh axis runs over, the one named last changes fastest.
Arguments:
- velocity: float32 [16, 128, 512], P('grp', 'slab'), may hold values from -6 to 6
- rate: float32 [16, 128, 512], P('grp', 'slab'), may hold values from 0.02 to 0.16
- forcing: float32 [16, 128, 512], P('grp', 'slab'), may hold values from -3 to 3
- anchor_line: int32 [512], P(('grp', 'slab')), may hold values from 0 to 63
- anchor_z: int32 [512], P(('grp', 'slab')), may hold values from 0 to 384
- assign: int32 [512, 1], P(('grp', 'slab')), may hold values from 0 to 15; in each aligned block of 16 rows (0 to 15, 16 to 31, ...) at most 2 rows name the same one
- spectral: float32 [2048, 64], replicated, may hold values from -0.75 to 0.75
- dense: float32 [68, 64], replicated, may hold values from -4 to 4
- momentum: float32 [2048, 64], P(('grp', 'slab')), may hold values from -0.3125 to 0.3125
Outputs:
- field_out: float32 [16, 128, 512], P('grp', 'slab')
- trainer_loss: float32 [2, 16], P('grp', 'slab')
- spectral_new: float32 [2048, 64], replicated
- dense_new: float32 [68, 64], replicated
- momentum_new: float32 [2048, 64], P(('grp', 'slab'))
The draws below stay inside these ranges and needn't reach their ends.
Inputs may be any that keep to these rules, and one draw needn't show every extreme that they name: `assign`: within the 16 lines of one device no trainer is named more than 2 times, and in some device's lines one trainer is named exactly 2 times.
All inputs are finite; a program needn't handle non-finite values.
Results may differ from the reference program's by a relative error of at most 0.0001.
Values sent between devices are 32-bit elements; how exact they have to be, the bound alone decides.
No kernel may reach another device: no remote copies, remote signals or barrier semaphores. Data moves between devices by JAX's collectives and lax.ppermute only.
A program may use at most 64 MiB of HBM per device.

```python
import math
import jax
import jax.numpy as jnp
import numpy as np
from jax import lax

CX = 8
CY = 8
CZ = 512
ROWS = 16
STEPS = 2
SUB = 128
MODES = 16
WIDTH = 64
CAP = 2
NX = 16
NY = 128
TOTAL = 512
N_GRP = 2
N_SLAB = 16


def place_ends(drawn, rng, low, largest):
    index_at = [jax.random.randint(jax.random.fold_in(rng, axis), (), 0, length) for axis, length in enumerate(drawn.shape)]
    longest = drawn.shape.index(max(drawn.shape))
    beside = index_at[:longest] + [(index_at[longest] + 1) % drawn.shape[longest]] + index_at[longest + 1:]
    return drawn.at[tuple(index_at)].set(low).at[tuple(beside)].set(largest)


def block_levels(rng, dims, shards, smallest, top_value):
    def one(position, blocks):
        steps = jax.random.uniform(jax.random.fold_in(jax.random.fold_in(rng, 6), position), (blocks,), jnp.float32, smallest / len(shards), top_value / len(shards))
        return jnp.repeat(jnp.exp(steps), dims[position] // blocks).reshape((-1,) + (1,) * (len(dims) - position - 1))

    factor_of = one(*shards[0])
    for cut in shards[1:]:
        factor_of = factor_of * one(*cut)
    return factor_of


def deal_out(stream_key, own, number, rows, count, top, limit, slope):
    ranking = jax.random.permutation(stream_key, count)
    crowded, usual = portions_of(count, rows * top, limit, slope, True), portions_of(count, rows * top, limit, slope, False)
    places = jnp.arange(count)

    def named(tallies, offset_by):
        used = int((tallies > 0).sum())
        fixed = max(1, used // 4)
        shifted = fixed + (places - fixed + offset_by * (used - fixed)) % max(1, count - fixed)
        return jnp.zeros((count,), jnp.int32).at[ranking[jnp.where(places < fixed, places, shifted)]].set(jnp.asarray(tallies, jnp.int32))

    tallies = jnp.where(number % 4 == 0, named(crowded, number // 4), named(usual, number - number // 4 - 1))
    mixed = jax.random.permutation(jax.random.fold_in(own, 3), count)
    giver, taker = mixed[0:count // 2 * 2:2], mixed[1:count // 2 * 2:2]
    margin = jnp.minimum(tallies[giver] - 1, limit - tallies[taker]) // 2
    margin = jnp.where((giver == ranking[0]) | (taker == ranking[0]) | (tallies[taker] == 0), 0, jnp.maximum(margin, 0))
    shifted = jax.random.randint(jax.random.fold_in(own, 4), (count // 2,), 0, 1 << 20) % (margin + 1)
    tallies = tallies.at[giver].add(-shifted).at[taker].add(shifted)
    items = jnp.searchsorted(jnp.cumsum(tallies), jnp.arange(rows * top), side="right").astype(jnp.int32)
    table = items.reshape(top, rows).T
    table = table[jax.random.permutation(jax.random.fold_in(own, 1), rows)]
    offset_by = jax.random.randint(jax.random.fold_in(own, 2), (rows, 1), 0, top)
    return jnp.take_along_axis(table, (jnp.arange(top)[None, :] + offset_by) % top, axis=1)


def portions_of(amount, total, reach, lean, full):
    portions = [(1 << 20) // math.isqrt(standing ** lean) + 1 for standing in range(1, amount + 1)]
    largest = reach if full else min(reach, max(-(-total // amount), total * portions[0] // sum(portions)))
    least = 1 if total - largest >= amount - 1 else 0
    given, spare = [largest] + [least] * (amount - 1), total - largest - least * (amount - 1)
    while spare > 0:
        free = [i for i in range(1, amount) if given[i] < largest] or [i for i in range(1, amount) if given[i] < reach]
        whole, remaining = sum([portions[i] for i in free]), spare
        for i in free:
            extra = min(reach - given[i], max(1, remaining * portions[i] // whole), spare)
            given[i] = given[i] + extra
            spare = spare - extra
    return np.array(given)


def centred(rng, extent, scale, limit, cuts=(), kind=jnp.bfloat16):
    factor_of = block_levels(rng, extent, cuts, -0.22, 0.18) if cuts else 1.0
    drawn = jax.random.normal(rng, extent, jnp.float32) * scale * factor_of
    return jnp.minimum(jnp.maximum(drawn, -limit), limit).astype(kind)


def setup_inputs(seed: int = 0) -> dict:
    seeds = jax.random.split(jax.random.key(seed), 10)
    velocity = centred(seeds[0], (NX, NY, CZ), 1.0, 6.0, ((0, 2), (1, 16)), jnp.float32)
    rate = jnp.clip(jnp.exp(math.log(0.16) - 2.0794415 * jax.random.uniform(seeds[1], (NX, NY, CZ), jnp.float32) ** block_levels(seeds[1], (NX, NY, CZ), ((0, 2), (1, 16)), -0.2, 0.2)), 0.02, 0.16)
    forcing = centred(seeds[2], (NX, NY, CZ), 0.2, 3.0, ((0, 2), (1, 16)), jnp.float32)
    anchor_line = place_ends(jax.random.randint(seeds[3], (TOTAL,), 0, CX * CY), jax.random.fold_in(seeds[3], 1), 0, (CX * CY) - 1).astype(jnp.int32)
    anchor_z = place_ends(jax.random.randint(seeds[4], (TOTAL,), 0, CZ - SUB + 1), jax.random.fold_in(seeds[4], 1), 0, CZ - SUB).astype(jnp.int32)
    assign_keys = jax.random.split(jax.random.fold_in(seeds[5], 1), TOTAL // ROWS)
    assign_turns = jax.random.permutation(jax.random.fold_in(seeds[5], 3), TOTAL // ROWS)
    assign = jax.vmap(lambda own, number: deal_out(jax.random.fold_in(seeds[5], 2), own, number, ROWS, N_SLAB, 1, CAP, 2))(assign_keys, assign_turns).reshape((TOTAL, 1))
    spectral = centred(seeds[6], (2 * MODES * WIDTH, WIDTH), WIDTH ** -0.5, 0.75, (), jnp.float32)
    dense = centred(seeds[7], (WIDTH + 4, WIDTH), 0.3, 4.0, (), jnp.float32)
    momentum = centred(seeds[8], (2 * MODES * WIDTH, WIDTH), 0.02, 0.3125, ((0, 32),), jnp.float32)
    return dict(velocity=velocity, rate=rate, forcing=forcing, anchor_line=anchor_line, anchor_z=anchor_z, assign=assign, spectral=spectral, dense=dense, momentum=momentum)


decay_rate = 0.9
learn_rate = 0.5
dense_rate = 3.0

def tendency_of(field_now, rate, forcing):
    padded = jnp.pad(field_now, ((1, 1), (1, 1), (0, 0)))
    beside = padded[2:, 1:-1] + padded[:-2, 1:-1] + padded[1:-1, 2:] + padded[1:-1, :-2]
    beside = beside + jnp.roll(field_now, 1, 2) + jnp.roll(field_now, -1, 2)
    return rate * (beside - 6.0 * field_now) + forcing

def tables():
    counts = jnp.arange(SUB, dtype=jnp.int32)
    waves = jnp.arange(MODES, dtype=jnp.int32)
    phase = counts[:, None] * waves[None, :] % SUB
    angle = phase.astype(jnp.float32) * (2.0 * jnp.pi / SUB)
    weight_k = jnp.where(waves == 0, 1.0, 2.0).astype(jnp.float32) / SUB
    return (jnp.cos(angle), jnp.sin(angle), weight_k)

def line_errors(spectral, dense, inputs, targets, valid):
    highest = lax.Precision.HIGHEST
    width = dense.shape[1]
    mixing = dense[:width]
    lift_gain, lift_bias, layer_bias, projection = (dense[width], dense[width + 1], dense[width + 2], dense[width + 3])
    cosine, sine, weight_k = tables()
    hidden = inputs[:, None, :] * lift_gain[None, :, None] + lift_bias[None, :, None]
    real_in = jnp.einsum('bws,sk->bwk', hidden, cosine, precision=highest)
    imag_in = -jnp.einsum('bws,sk->bwk', hidden, sine, precision=highest)
    blocks = spectral.reshape(2, MODES, width, width)
    w_real, w_imag = (blocks[0], blocks[1])
    real_out = jnp.einsum('bwk,kwv->bvk', real_in, w_real, precision=highest) - jnp.einsum('bwk,kwv->bvk', imag_in, w_imag, precision=highest)
    imag_out = jnp.einsum('bwk,kwv->bvk', real_in, w_imag, precision=highest) + jnp.einsum('bwk,kwv->bvk', imag_in, w_real, precision=highest)
    spatial = jnp.einsum('bvk,sk->bvs', real_out * weight_k, cosine, precision=highest) - jnp.einsum('bvk,sk->bvs', imag_out * weight_k, sine, precision=highest)
    before = spatial + jnp.einsum('bws,wv->bvs', hidden, mixing, precision=highest) + layer_bias[None, :, None]
    after = jax.nn.gelu(before)
    output = jnp.einsum('bvs,v->bs', after, projection, precision=highest)
    return lax.optimization_barrier(jnp.sum((output - targets) ** 2, axis=1)) * valid

def reference(velocity, rate, forcing, anchor_line, anchor_z, assign, spectral, dense, momentum):
    field_now = velocity
    previous = velocity
    change = velocity
    for number in range(STEPS):
        previous = field_now
        change = tendency_of(field_now, rate, forcing)
        field_now = field_now + change
    lines = jnp.arange(TOTAL, dtype=jnp.int32)
    device = lines // ROWS
    grp_index = device // N_SLAB
    slab_index = device % N_SLAB
    first = grp_index * CX + anchor_line // CY
    second = slab_index * CY + anchor_line % CY
    windows = jax.vmap(lambda row, start: lax.dynamic_slice_in_dim(row, start, SUB))
    inputs = windows(previous[first, second], anchor_z.astype(jnp.int32))
    targets = windows(change[first, second], anchor_z.astype(jnp.int32))
    scale = 1.0 / (TOTAL * SUB)
    devices = TOTAL // ROWS
    inputs = inputs.reshape(devices, ROWS, SUB)
    targets = targets.reshape(devices, ROWS, SUB)

    def one_block(carry, pieces):
        block_in, block_tg = pieces

        def loss_fn(spec, dens):
            errors = line_errors(spec, dens, block_in, block_tg, jnp.ones((ROWS,), jnp.float32))
            return (jnp.sum(errors) * scale, errors)
        value, pullback, errors = jax.vjp(loss_fn, spectral, dense, has_aux=True)
        grad_spec, grad_dense = pullback(jnp.ones((), jnp.float32))
        return ((carry[0] + grad_spec, carry[1] + grad_dense), errors)
    start = (jnp.zeros_like(spectral), jnp.zeros_like(dense))
    (grad_spec, grad_dense), errors = lax.scan(one_block, start, (inputs, targets))
    errors = errors.reshape(TOTAL)
    trainer = grp_index * N_SLAB + assign[:, 0]
    onehot = (trainer[:, None] == jnp.arange(N_GRP * N_SLAB, dtype=jnp.int32)[None, :]).astype(jnp.float32)
    trainer_loss = jnp.dot(errors, onehot, precision=lax.Precision.HIGHEST) / (ROWS * SUB)
    momentum_new = decay_rate * momentum + grad_spec
    spectral_new = spectral - learn_rate * momentum_new
    dense_new = dense - dense_rate * grad_dense
    return (field_now, trainer_loss.reshape(N_GRP, N_SLAB), spectral_new, dense_new, momentum_new)
```

```python
import functools
import math

import jax
import jax.numpy as jnp
import numpy as np
from jax import lax
from jax.experimental import pallas as pl
from jax.experimental.pallas import tpu as pltpu
from jax.sharding import PartitionSpec as P

STEPS = 2
SUB = 128
MODES = 16
LANES = 128
FEATURES = 2 * MODES + 8

decay_rate = 0.9
learn_rate = 0.5
dense_rate = 3.0

AXES = ("grp", "slab")
HIGHEST = lax.Precision.HIGHEST
NT = (((1,), (1,)), ((), ()))
VMEM = pl.BlockSpec(memory_space=pltpu.VMEM)
SMEM = pl.BlockSpec(memory_space=pltpu.SMEM)


def call(kernel, outs, scratch=(), ins=(), aliases=None, flops=1000000):
    outs = [jax.ShapeDtypeStruct(shape, dtype) for shape, dtype in outs]
    size = sum(math.prod(o.shape) * o.dtype.itemsize for o in outs)
    return pl.pallas_call(
        kernel,
        out_shape=outs,
        in_specs=list(ins),
        out_specs=[VMEM] * len(outs),
        scratch_shapes=list(scratch),
        input_output_aliases=aliases or {},
        compiler_params=pltpu.CompilerParams(vmem_limit_bytes=16 << 20),
        cost_estimate=pl.CostEstimate(flops=flops, bytes_accessed=2 * size, transcendentals=0),
    )


def tables():
    counts = np.arange(SUB)
    waves = np.arange(MODES)
    angle = (waves[:, None] * counts[None, :] % SUB) * (2.0 * np.pi / SUB)
    weight = np.where(waves == 0, 1.0, 2.0)[:, None] / SUB
    cosine, sine = np.cos(angle), np.sin(angle)
    return np.concatenate([cosine, sine, weight * cosine, weight * sine]).astype(np.float32)


def put_plane(ref, row, plane):
    for q in range(plane.shape[1] // LANES):
        ref[row + 8 * q : row + 8 * q + 8, :] = plane[:, q * LANES : (q + 1) * LANES]


def get_plane(ref, row, chunks):
    return jnp.concatenate([ref[row + 8 * q : row + 8 * q + 8, :] for q in range(chunks)], axis=1)


def pack_rows(block):
    half = block.shape[0] // 2
    return jnp.concatenate([block[:half], block[half:]], axis=1)


def edge_kernel(side, with_momentum, v_ref, rate_ref, forcing_ref, momentum_ref, out_ref):
    last = v_ref.shape[0] - 1
    chunks = v_ref.shape[2] // LANES
    high = (lax.axis_index("grp") == 0) if side is None else side
    edge = jnp.where(high, last, 0)
    second = jnp.where(high, last - 1, 1)
    planes = (v_ref[edge], v_ref[second], rate_ref[edge], forcing_ref[edge])
    for number, plane in enumerate(planes):
        put_plane(out_ref, number * 8 * chunks, plane)
    if with_momentum:
        packed = pack_rows(momentum_ref[...])
        start = 4 * 8 * chunks
        out_ref[start : start + packed.shape[0], :] = packed


def grp_halo(two_sided, ref_low, ref_high, layer, chunks):
    rows = 8 * chunks * layer
    if two_sided:
        return get_plane(ref_low, rows, chunks), get_plane(ref_high, rows, chunks)
    plane = get_plane(ref_low, rows, chunks)
    first = lax.axis_index("grp") == 0
    return jnp.where(first, 0.0, plane), jnp.where(first, plane, 0.0)


def side_kernel(two_sided, packed_rows, v_ref, rate_ref, forcing_ref, low_ref, high_ref, own_ref, *outs):
    a_ref, b_ref = outs[:2]
    last = v_ref.shape[1] - 1
    chunks = v_ref.shape[2] // LANES
    even = lax.rem(lax.axis_index("slab"), 2) == 0
    columns = ((v_ref, 0), (v_ref, 1), (rate_ref, 0), (forcing_ref, 0))
    for number, (ref, offset) in enumerate(columns):
        left, right = ref[:, offset, :], ref[:, last - offset, :]
        put_plane(a_ref, number * 8 * chunks, jnp.where(even, right, left))
        put_plane(b_ref, number * 8 * chunks, jnp.where(even, left, right))
    low, high = grp_halo(two_sided, low_ref, high_ref, 0, chunks)
    start = 4 * 8 * chunks
    for number, plane in enumerate((low, high)):
        left, right = plane[0:1], plane[last : last + 1]
        to_a, to_b = jnp.where(even, right, left), jnp.where(even, left, right)
        for q in range(chunks):
            row = start + number * chunks + q
            a_ref[row : row + 1, :] = to_a[:, q * LANES : (q + 1) * LANES]
            b_ref[row : row + 1, :] = to_b[:, q * LANES : (q + 1) * LANES]
    if packed_rows:
        outs[2][0:packed_rows, :] = own_ref[start : start + packed_rows, :]
        outs[2][packed_rows : 2 * packed_rows, :] = low_ref[start : start + packed_rows, :]


def feature_kernel(width, spectral_ref, dense_ref, map_ref, gain_ref, bias_ref, projection_ref, square, rows):
    square[...] = jnp.zeros_like(square)
    square[0 : dense_ref.shape[0], 0:width] = dense_ref[...]
    turned = square[...].T
    gain = jnp.broadcast_to(turned[0:width, width : width + 1], (width, LANES))
    bias = jnp.broadcast_to(turned[0:width, width + 1 : width + 2], (width, LANES))
    gain_ref[...] = gain
    bias_ref[...] = bias
    projection_ref[...] = jnp.broadcast_to(turned[0:width, width + 3 : width + 4], (width, LANES))
    gain, bias = gain[:, :width], bias[:, :width]
    rows[...] = jnp.zeros_like(rows)
    for block in range(2 * MODES):
        weights = spectral_ref[block * width : (block + 1) * width, :]
        rows[block : block + 1, 0:width] = jnp.sum(gain * weights, axis=0, keepdims=True)
    mixing = dense_ref[0:width, :]
    rows[2 * MODES : 2 * MODES + 1, 0:width] = jnp.sum(gain * mixing, axis=0, keepdims=True)
    rows[2 * MODES + 1 : 2 * MODES + 2, 0:width] = (
        jnp.sum(bias * (mixing + spectral_ref[0:width, :]), axis=0, keepdims=True)
        + dense_ref[width + 2 : width + 3, :]
    )
    full = rows[0:FEATURES, :]
    coarse = full.astype(jnp.bfloat16).astype(jnp.float32)
    rows[0:FEATURES, :] = coarse
    rows[FEATURES : 2 * FEATURES, :] = coarse
    rows[2 * FEATURES : 3 * FEATURES, :] = full - coarse
    map_ref[...] = rows[...].T[0:width, :].astype(jnp.bfloat16)


def step_kernel(
    two_sided, width, pay_rows, scale, v_ref, rate_ref, forcing_ref, low_ref, high_ref, a_ref, b_ref,
    line_ref, start_ref, assign_ref, map_ref, projection_ref, table_ref,
    field_ref, pay_ref, previous, change, inputs_ref, targets_ref, feature_ref, slope_ref,
):
    cells_x, cells_y, cells_z = v_ref.shape
    chunks = cells_z // LANES
    even = lax.rem(lax.axis_index("slab"), 2) == 0

    def grp_layer(layer):
        return grp_halo(two_sided, low_ref, high_ref, layer, chunks)

    def slab_layer(layer):
        from_a = get_plane(a_ref, 8 * chunks * layer, chunks)
        from_b = get_plane(b_ref, 8 * chunks * layer, chunks)
        return jnp.where(even, from_b, from_a), jnp.where(even, from_a, from_b)

    def corner(number):
        start = 4 * 8 * chunks + number * chunks
        from_a = jnp.concatenate([a_ref[start + q : start + q + 1, :] for q in range(chunks)], axis=1)
        from_b = jnp.concatenate([b_ref[start + q : start + q + 1, :] for q in range(chunks)], axis=1)
        return jnp.where(even, from_b, from_a), jnp.where(even, from_a, from_b)

    sublane = lax.broadcasted_iota(jnp.int32, (8, cells_z), 0)

    def shifted(plane, before, after):
        up = jnp.where(sublane == 7, after, pltpu.roll(plane, 7, 0))
        down = jnp.where(sublane == 0, before, pltpu.roll(plane, 1, 0))
        return up, down

    def tendency(plane, above, below, up, down, rate, forcing):
        beside = above + below + up + down
        beside = beside + pltpu.roll(plane, 1, 1) + pltpu.roll(plane, cells_z - 1, 1)
        return rate * (beside - 6.0 * plane) + forcing

    low1, high1 = grp_layer(0)
    low2, high2 = grp_layer(1)
    low_rate, high_rate = grp_layer(2)
    low_force, high_force = grp_layer(3)
    left1, right1 = slab_layer(0)
    left2, right2 = slab_layer(1)
    left_rate, right_rate = slab_layer(2)
    left_force, right_force = slab_layer(3)
    low_left, low_right = corner(0)
    high_left, high_right = corner(1)

    planes = [low2, low1] + [v_ref[i] for i in range(cells_x)] + [high1, high2]
    rates = [low_rate] + [rate_ref[i] for i in range(cells_x)] + [high_rate]
    forces = [low_force] + [forcing_ref[i] for i in range(cells_x)] + [high_force]
    lefts = [low_left] + [left1[i : i + 1] for i in range(cells_x)] + [high_left]
    rights = [low_right] + [right1[i : i + 1] for i in range(cells_x)] + [high_right]
    stepped = []
    for i in range(cells_x + 2):
        plane = planes[i + 1]
        up, down = shifted(plane, lefts[i], rights[i])
        stepped.append(plane + tendency(plane, planes[i + 2], planes[i], up, down, rates[i], forces[i]))

    def column_step(near, far, inner, rate, forcing, low, high):
        above, below = shifted(near, low, high)
        return near + tendency(near, above, below, inner, far, rate, forcing)

    left_inner = v_ref[:, 0, :]
    right_inner = v_ref[:, cells_y - 1, :]
    left_new = column_step(left1, left2, left_inner, left_rate, left_force, low_left, high_left)
    right_new = column_step(right1, right2, right_inner, right_rate, right_force, low_right, high_right)
    for i in range(cells_x):
        plane = stepped[i + 1]
        up, down = shifted(plane, left_new[i : i + 1], right_new[i : i + 1])
        moved = tendency(plane, stepped[i + 2], stepped[i], up, down, rate_ref[i], forcing_ref[i])
        field_ref[i] = plane + moved
        previous[8 * i : 8 * i + 8, 0:cells_z] = plane
        change[8 * i : 8 * i + 8, 0:cells_z] = moved
    count = line_ref.shape[0]
    previous[:, cells_z : cells_z + LANES] = jnp.zeros((8 * cells_x, LANES), jnp.float32)
    change[:, cells_z : cells_z + LANES] = jnp.zeros((8 * cells_x, LANES), jnp.float32)
    for t in range(count):
        line, start = line_ref[t], start_ref[t]
        base = pl.multiple_of((start // LANES) * LANES, LANES)
        turn = lax.rem(2 * LANES - lax.rem(start, LANES), 2 * LANES)
        row = previous[pl.ds(line, 1), pl.ds(base, 2 * LANES)]
        inputs_ref[t : t + 1, :] = pltpu.roll(row, turn, 1)[:, :SUB]
        row = change[pl.ds(line, 1), pl.ds(base, 2 * LANES)]
        targets_ref[t : t + 1, :] = pltpu.roll(row, turn, 1)[:, :SUB]

    table = table_ref[...]
    cos_w, sin_w = table[2 * MODES : 3 * MODES], table[3 * MODES :]
    inputs = inputs_ref[...]
    waves = lax.dot_general(
        table[: 2 * MODES], inputs, NT, precision=HIGHEST, preferred_element_type=jnp.float32
    )
    tail = lax.broadcasted_iota(jnp.int32, (8, SUB), 0)
    projection = projection_ref[...]
    channel_map = map_ref[...]
    held = jnp.zeros((width, SUB), jnp.float32)
    lane = lax.broadcasted_iota(jnp.int32, (1, LANES), 1)
    losses = jnp.zeros((1, LANES), jnp.float32)
    root = math.sqrt(2.0 / math.pi)
    for t in range(count):
        real, imag = waves[:MODES, t : t + 1], waves[MODES:, t : t + 1]
        line = inputs_ref[t : t + 1, :]
        rest = jnp.where(tail == 0, line, jnp.where(tail == 1, 1.0, 0.0))
        feature = jnp.concatenate([real * cos_w + imag * sin_w, imag * cos_w - real * sin_w, rest], axis=0)
        coarse = feature.astype(jnp.bfloat16).astype(jnp.float32)
        fine = feature - coarse
        zeros = jnp.zeros((LANES - 3 * FEATURES, SUB), jnp.float32)
        stack = jnp.concatenate([coarse, fine, coarse, zeros], axis=0).astype(jnp.bfloat16)
        feature_ref[:, t * SUB : (t + 1) * SUB] = stack
        before = jnp.dot(channel_map, stack, preferred_element_type=jnp.float32)
        square = before * before
        bend = jnp.tanh(root * (before + 0.044715 * (before * square)))
        half = 0.5 * (1.0 + bend)
        after = before * half
        slope = half + (0.5 * root) * before * (1.0 - bend * bend) * (1.0 + (3 * 0.044715) * square)
        output = jnp.sum(after * projection, axis=0, keepdims=True)
        differ = output - targets_ref[t : t + 1, :]
        error = jnp.sum(differ * differ, axis=1, keepdims=True)
        losses = losses + jnp.where(lane == assign_ref[t], error, 0.0)
        pull = (2.0 * scale) * differ
        held = held + after * pull
        slope = slope * projection * pull
        coarse = slope.astype(jnp.bfloat16).astype(jnp.float32)
        slope_ref[0:width, t * SUB : (t + 1) * SUB] = coarse.astype(jnp.bfloat16)
        slope_ref[width : 2 * width, t * SUB : (t + 1) * SUB] = (slope - coarse).astype(jnp.bfloat16)
    pairs = lax.dot_general(
        feature_ref[...], slope_ref[...], NT, preferred_element_type=jnp.float32
    )
    total = pairs[0:FEATURES, 0:width] + pairs[FEATURES : 2 * FEATURES, 0:width] + pairs[0:FEATURES, width:]
    pay_ref[...] = jnp.zeros_like(pay_ref)
    pay_ref[0:MODES, :] = jnp.concatenate([total[0:MODES], total[MODES : 2 * MODES]], axis=1)
    row = 2 * MODES
    pay_ref[MODES : MODES + 1, :] = jnp.concatenate([total[row : row + 1], total[row + 1 : row + 2]], axis=1)
    ones = jnp.ones((8, SUB), jnp.float32)
    summed = lax.dot_general(ones, held, NT, precision=HIGHEST, preferred_element_type=jnp.float32)
    pay_ref[MODES + 1 : MODES + 2, 0:width] = summed[0:1]
    pay_ref[pl.ds(MODES + 2 + lax.axis_index("grp"), 1), :] = losses


def base_kernel(masks, width, spectral_ref, mine_ref, other_ref, out_ref):
    here = lax.axis_index("grp") * lax.axis_size("slab") + lax.axis_index("slab")
    rows = width // 2
    held = mine_ref.shape[0] // rows
    for number in range(2 * held):
        source = here
        for bit, mask in enumerate(masks):
            if number >> bit & 1:
                source = source ^ mask
        ref, place = (mine_ref, number) if number < held else (other_ref, number - held)
        for part in range(2):
            start = pl.multiple_of(source * width + part * rows, rows)
            moved = ref[place * rows : (place + 1) * rows, part * width : (part + 1) * width]
            out_ref[pl.ds(start, rows), :] = spectral_ref[pl.ds(start, rows), :] - (learn_rate * decay_rate) * moved


def update_kernel(
    width, lines, pay_ref, spectral_ref, base_ref, dense_ref, momentum_ref, gain_ref, bias_ref,
    spectral_out, dense_out, momentum_out, loss_out, row_ref,
):
    first, second = lax.axis_index("grp"), lax.axis_index("slab")
    here = first * lax.axis_size("slab") + second
    gain, bias = gain_ref[:, 0:width], bias_ref[:, 0:width]
    row_ref[0:MODES, :] = pay_ref[0:MODES, 0:width]
    row_ref[MODES : 2 * MODES, :] = pay_ref[0:MODES, width : 2 * width]
    slopes = pay_ref[MODES : MODES + 2, :]
    by_input, by_one = slopes[0:1, 0:width], slopes[0:1, width : 2 * width]
    offset = bias * by_one
    gathered = dense_ref[0:width, :] * by_input
    for block in range(2 * MODES):
        span = slice(block * width, (block + 1) * width)
        row = row_ref[block : block + 1, :]
        gradient = gain * row
        if block == 0:
            gradient = gradient + offset
        spectral_out[span, :] = base_ref[span, :] - learn_rate * gradient
        gathered = gathered + spectral_ref[span, :] * row
    constant = (dense_ref[0:width, :] + spectral_ref[0:width, :]) * by_one
    ones = jnp.ones((8, width), jnp.float32)
    gain_row = lax.dot_general(ones, gathered, NT, precision=HIGHEST, preferred_element_type=jnp.float32)
    bias_row = lax.dot_general(ones, constant, NT, precision=HIGHEST, preferred_element_type=jnp.float32)
    dense_out[0:width, :] = dense_ref[0:width, :] - dense_rate * (gain * by_input + offset)
    changes = (gain_row[0:1], bias_row[0:1], by_one, slopes[1:2, 0:width])
    for number, gradient in enumerate(changes):
        at = slice(width + number, width + number + 1)
        dense_out[at, :] = dense_ref[at, :] - dense_rate * gradient
    piece = momentum_ref.shape[0]
    block = here * piece // width
    inside = 0 if piece == width else pl.multiple_of(lax.rem(here * piece, width), piece)
    at = pl.ds(inside, piece)
    gradient = gain_ref[at, 0:width] * row_ref[pl.ds(block, 1), :]
    gradient = gradient + jnp.where(block == 0, bias_ref[at, 0:width] * by_one, 0.0)
    momentum_out[...] = decay_rate * momentum_ref[...] + gradient
    sums = pay_ref[pl.ds(MODES + 2 + first, 1), :]
    lane = lax.broadcasted_iota(jnp.int32, (1, LANES), 1)
    own = jnp.sum(jnp.where(lane == second, sums, 0.0), axis=1, keepdims=True)
    loss_out[...] = own * (1.0 / (lines * SUB))


def hop_masks(n_grp, n_slab):
    masks, bit = [], 0
    while 1 << bit < n_slab:
        masks.append(3 << (bit - 1) if bit > 2 and bit % 2 else 1 << bit)
        bit += 1
    bit = 1
    while bit < n_grp:
        masks.append(bit * n_slab)
        bit *= 2
    return masks


def swap(array, mask, count):
    return lax.ppermute(array, AXES, [(i, i ^ mask) for i in range(count)])


def local(velocity, rate, forcing, anchor_line, anchor_z, assign, spectral, dense, momentum):
    n_grp, n_slab = lax.axis_size("grp"), lax.axis_size("slab")
    devices = n_grp * n_slab
    width = dense.shape[1]
    lines = anchor_line.shape[0]
    cells_x, cells_y, cells_z = velocity.shape
    chunks = cells_z // LANES
    halo_rows = 4 * 8 * chunks
    piece = momentum.shape[0]
    packed = piece // 2
    f32 = jnp.float32
    joined = n_grp == 2 and piece == width and devices & (devices - 1) == 0
    two_sided = n_grp != 2
    table = jnp.asarray(tables())

    def edge(side):
        rows = halo_rows + (packed if joined else 0)
        return call(
            functools.partial(edge_kernel, side, joined), [((rows, LANES), f32)], ins=[VMEM] * 4
        )(velocity, rate, forcing, momentum)[0]

    if two_sided:
        low = lax.ppermute(edge(True), "grp", [(i, i + 1) for i in range(n_grp - 1)])
        high = lax.ppermute(edge(False), "grp", [(i + 1, i) for i in range(n_grp - 1)])
        own = low
    else:
        own = edge(None)
        low = high = lax.ppermute(own, "grp", [(0, 1), (1, 0)])
    message = (halo_rows + 2 * chunks, LANES)
    outs = [(message, f32), (message, f32)] + ([((2 * packed, LANES), f32)] if joined else [])
    to_a, to_b, *gathered = call(
        functools.partial(side_kernel, two_sided, packed if joined else 0), outs, ins=[VMEM] * 6
    )(velocity, rate, forcing, low, high, own)
    pairs = [(i, i ^ 1) for i in range(n_slab)]
    odd = [(i, i + 1) for i in range(1, n_slab - 1, 2)]
    from_b = lax.ppermute(to_b, "slab", odd + [(j, i) for i, j in odd])
    from_a = lax.ppermute(to_a, "slab", pairs)

    channel_map, gain, bias, projection = call(
        functools.partial(feature_kernel, width),
        [((width, LANES), jnp.bfloat16)] + [((width, LANES), f32)] * 3,
        scratch=[pltpu.VMEM((LANES, LANES), f32), pltpu.VMEM((LANES, LANES), f32)],
        ins=[VMEM] * 2,
    )(spectral, dense)
    pay_rows = -(-(MODES + 2 + n_grp) // 8) * 8
    scale = 1.0 / (devices * lines * SUB)
    field_now, payload = call(
        functools.partial(step_kernel, two_sided, width, pay_rows, scale),
        [(velocity.shape, f32), ((pay_rows, LANES), f32)],
        scratch=[
            pltpu.VMEM((8 * cells_x, cells_z + LANES), f32),
            pltpu.VMEM((8 * cells_x, cells_z + LANES), f32),
            pltpu.VMEM((lines, SUB), f32),
            pltpu.VMEM((lines, SUB), f32),
            pltpu.VMEM((LANES, lines * SUB), jnp.bfloat16),
            pltpu.VMEM((2 * width, lines * SUB), jnp.bfloat16),
        ],
        ins=[VMEM] * 7 + [SMEM] * 3 + [VMEM] * 3,
    )(velocity, rate, forcing, low, high, from_a, from_b,
      anchor_line, anchor_z, assign.reshape(-1), channel_map, projection, table)

    masks = hop_masks(n_grp, n_slab)
    if joined:
        mine = gathered[0]
        order = [n_slab] + [m for m in masks if m not in (1, n_slab)] + [1]
        for mask in order[1:-1]:
            mine = jnp.concatenate([mine, swap(mine, mask, devices)], axis=0)
        other = swap(mine, order[-1], devices)
        base = call(
            functools.partial(base_kernel, order, width), [(spectral.shape, f32)], ins=[VMEM] * 3
        )(spectral, mine, other)[0]
    else:
        whole = lax.all_gather(momentum, AXES, axis=0, tiled=True)
        base = spectral - (learn_rate * decay_rate) * whole
    if devices & (devices - 1) == 0:
        for mask in masks:
            payload = payload + swap(payload, mask, devices)
    else:
        payload = lax.psum(payload, AXES)
    spectral_new, dense_new, momentum_new, trainer_loss = call(
        functools.partial(update_kernel, width, lines),
        [(spectral.shape, f32), (dense.shape, f32), (momentum.shape, f32), ((1, 1), f32)],
        scratch=[pltpu.VMEM((2 * MODES, width), f32)],
        ins=[VMEM] * 7,
    )(payload, spectral, base, dense, momentum, gain, bias)
    return (field_now, trainer_loss, spectral_new, dense_new, momentum_new)


def solution(mesh):
    placed = (
        P("grp", "slab", None),
        P("grp", "slab", None),
        P("grp", "slab", None),
        P(("grp", "slab")),
        P(("grp", "slab")),
        P(("grp", "slab"), None),
        P(),
        P(),
        P(("grp", "slab"), None),
    )
    return jax.shard_map(
        local,
        mesh=mesh,
        in_specs=placed,
        out_specs=(P("grp", "slab", None), P("grp", "slab"), P(), P(), P(("grp", "slab"), None)),
        check_vma=False,
    )
```

```python
import functools
import math

import jax
import jax.numpy as jnp
import numpy as np
from jax import lax
from jax.experimental import pallas as pl
from jax.experimental.pallas import tpu as pltpu
from jax.sharding import PartitionSpec as P


SUB = 128
MODES = 16
LANES = 128
FEATURES = 2 * MODES + 8

decay_rate = 0.9
learn_rate = 0.5
dense_rate = 3.0

AXES = ("grp", "slab")
HIGHEST = lax.Precision.HIGHEST
NT = (((1,), (1,)), ((), ()))
VMEM = pl.BlockSpec(memory_space=pltpu.VMEM)
HBM = pl.BlockSpec(memory_space=pltpu.HBM)


def call(kernel, outs, scratch=(), ins=(), places=None, flops=1000000):
    outs = [jax.ShapeDtypeStruct(shape, dtype) for shape, dtype in outs]
    size = sum(math.prod(o.shape) * o.dtype.itemsize for o in outs)
    return pl.pallas_call(
        kernel,
        out_shape=outs,
        in_specs=list(ins),
        out_specs=places or [VMEM] * len(outs),
        scratch_shapes=list(scratch),
        compiler_params=pltpu.CompilerParams(vmem_limit_bytes=16 << 20),
        cost_estimate=pl.CostEstimate(flops=flops, bytes_accessed=2 * size, transcendentals=0),
    )


def tables():
    counts = np.arange(SUB)
    waves = np.arange(MODES)
    angle = (waves[:, None] * counts[None, :] % SUB) * (2.0 * np.pi / SUB)
    weight = np.where(waves == 0, 1.0, 2.0)[:, None] / SUB
    cosine, sine = np.cos(angle), np.sin(angle)
    return np.concatenate([cosine, sine, weight * cosine, weight * sine]).astype(np.float32)


def put_plane(ref, row, plane):
    for q in range(plane.shape[1] // LANES):
        ref[row + 8 * q : row + 8 * q + 8, :] = plane[:, q * LANES : (q + 1) * LANES]


def get_plane(ref, row, chunks):
    return jnp.concatenate([ref[row + 8 * q : row + 8 * q + 8, :] for q in range(chunks)], axis=1)


def pack_rows(block):
    half = block.shape[0] // 2
    return jnp.concatenate([block[:half], block[half:]], axis=1)


def edge_kernel(
    with_momentum, v_hbm, rate_hbm, forcing_hbm, momentum_hbm, v_ref, rate_ref, forcing_ref, momentum_ref, *rest
):
    out_refs, sems = rest[:-1], rest[-1]
    moves = [
        pltpu.make_async_copy(source, target, sems.at[number])
        for number, (source, target) in enumerate(
            ((momentum_hbm, momentum_ref), (v_hbm, v_ref), (rate_hbm, rate_ref), (forcing_hbm, forcing_ref))
        )
    ]
    for move in moves:
        move.start()
    last = v_ref.shape[0] - 1
    chunks = v_ref.shape[2] // LANES
    moves[0].wait()
    if with_momentum:
        packed = pack_rows(momentum_ref[...].T)
        start = 4 * 8 * chunks
        out_refs[0][start : start + packed.shape[0], :] = packed
    for move in moves[1:]:
        move.wait()
    sides = [lax.axis_index("grp") == 0] if len(out_refs) == 1 else [True, False]
    for out_ref, high in zip(out_refs, sides):
        edge = jnp.where(high, last, 0)
        second = jnp.where(high, last - 1, 1)
        planes = (v_ref[edge], v_ref[second], rate_ref[edge], forcing_ref[edge])
        for number, plane in enumerate(planes):
            put_plane(out_ref, number * 8 * chunks, plane)


def grp_halo(two_sided, ref_low, ref_high, layer, chunks):
    rows = 8 * chunks * layer
    if two_sided:
        return get_plane(ref_low, rows, chunks), get_plane(ref_high, rows, chunks)
    plane = get_plane(ref_low, rows, chunks)
    first = lax.axis_index("grp") == 0
    return jnp.where(first, 0.0, plane), jnp.where(first, plane, 0.0)


def side_kernel(two_sided, packed_rows, v_ref, rate_ref, forcing_ref, low_ref, high_ref, own_ref, *outs):
    a_ref, b_ref = outs[:2]
    last = v_ref.shape[1] - 1
    chunks = v_ref.shape[2] // LANES
    even = lax.rem(lax.axis_index("slab"), 2) == 0
    columns = ((v_ref, 0), (v_ref, 1), (rate_ref, 0), (forcing_ref, 0))
    for number, (ref, offset) in enumerate(columns):
        left, right = ref[:, offset, :], ref[:, last - offset, :]
        put_plane(a_ref, number * 8 * chunks, jnp.where(even, right, left))
        put_plane(b_ref, number * 8 * chunks, jnp.where(even, left, right))
    low, high = grp_halo(two_sided, low_ref, high_ref, 0, chunks)
    start = 4 * 8 * chunks
    for number, plane in enumerate((low, high)):
        left, right = plane[0:1], plane[last : last + 1]
        to_a, to_b = jnp.where(even, right, left), jnp.where(even, left, right)
        for q in range(chunks):
            row = start + number * chunks + q
            a_ref[row : row + 1, :] = to_a[:, q * LANES : (q + 1) * LANES]
            b_ref[row : row + 1, :] = to_b[:, q * LANES : (q + 1) * LANES]
    if packed_rows:
        outs[2][0:packed_rows, :] = own_ref[start : start + packed_rows, :]
        outs[2][packed_rows : 2 * packed_rows, :] = low_ref[start : start + packed_rows, :]


def as_row(column):
    size = column.shape[0]
    square = (size, size)
    same = lax.broadcasted_iota(jnp.int32, square, 0) == lax.broadcasted_iota(jnp.int32, square, 1)
    return jnp.sum(jnp.where(same, column, 0.0), axis=0, keepdims=True)


def as_column(row):
    size = row.shape[1]
    square = (size, size)
    same = lax.broadcasted_iota(jnp.int32, square, 0) == lax.broadcasted_iota(jnp.int32, square, 1)
    return jnp.sum(jnp.where(same, row, 0.0), axis=1, keepdims=True)


def feature_kernel(width, spectral_ref, dense_ref, map_ref, projection_ref, row_ref):
    gain = as_row(dense_ref[:, width : width + 1])
    bias = as_row(dense_ref[:, width + 1 : width + 2])
    projection_ref[...] = jnp.broadcast_to(dense_ref[:, width + 3 : width + 4], (width, LANES))
    row_ref[...] = jnp.zeros_like(row_ref)
    row_ref[0:1, :] = jnp.concatenate([gain, gain], axis=1)
    row_ref[1:2, :] = jnp.concatenate([bias, bias], axis=1)
    gains = row_ref[0:1, :]
    lane = lax.broadcasted_iota(jnp.int32, (width, LANES), 1)
    low = lane < width
    full = jnp.zeros((width, LANES), jnp.float32)
    for pair in range(MODES):
        product = spectral_ref[:, pair * LANES : (pair + 1) * LANES] * gains
        first = jnp.sum(jnp.where(low, product, 0.0), axis=1, keepdims=True)
        second = jnp.sum(jnp.where(low, 0.0, product), axis=1, keepdims=True)
        full = jnp.where(lane == 2 * pair, first, jnp.where(lane == 2 * pair + 1, second, full))
    mixing = dense_ref[:, 0:width]
    by_input = jnp.sum(gain * mixing, axis=1, keepdims=True)
    by_one = jnp.sum(bias * (mixing + spectral_ref[:, 0:width]), axis=1, keepdims=True)
    by_one = by_one + dense_ref[:, width + 2 : width + 3]
    full = jnp.where(lane == 2 * MODES, by_input, jnp.where(lane == 2 * MODES + 1, by_one, full))
    coarse = full.astype(jnp.bfloat16).astype(jnp.float32)
    fine = full - coarse
    joined = coarse + pltpu.roll(coarse, FEATURES, 1) + pltpu.roll(fine, 2 * FEATURES, 1)
    map_ref[...] = joined.astype(jnp.bfloat16)


def step_kernel(
    two_sided, width, scale, v_ref, rate_ref, forcing_ref, low_ref, high_ref, a_ref, b_ref,
    line_hbm, start_hbm, assign_hbm, map_ref, projection_ref, table_ref,
    previous, change, pay_ref, line_ref, start_ref, assign_ref, sems,
    inputs_ref, targets_ref, feature_ref, slope_ref,
):
    moves = [
        pltpu.make_async_copy(source, target, sems.at[number])
        for number, (source, target) in enumerate(
            ((line_hbm, line_ref), (start_hbm, start_ref), (assign_hbm, assign_ref))
        )
    ]
    for move in moves:
        move.start()
    cells_x, cells_y, cells_z = v_ref.shape
    chunks = cells_z // LANES
    even = lax.rem(lax.axis_index("slab"), 2) == 0

    def grp_layer(layer):
        return grp_halo(two_sided, low_ref, high_ref, layer, chunks)

    def slab_layer(layer):
        from_a = get_plane(a_ref, 8 * chunks * layer, chunks)
        from_b = get_plane(b_ref, 8 * chunks * layer, chunks)
        return jnp.where(even, from_b, from_a), jnp.where(even, from_a, from_b)

    def corner(number):
        start = 4 * 8 * chunks + number * chunks
        from_a = jnp.concatenate([a_ref[start + q : start + q + 1, :] for q in range(chunks)], axis=1)
        from_b = jnp.concatenate([b_ref[start + q : start + q + 1, :] for q in range(chunks)], axis=1)
        return jnp.where(even, from_b, from_a), jnp.where(even, from_a, from_b)

    sublane = lax.broadcasted_iota(jnp.int32, (8, cells_z), 0)

    def shifted(plane, before, after):
        up = jnp.where(sublane == 7, after, pltpu.roll(plane, 7, 0))
        down = jnp.where(sublane == 0, before, pltpu.roll(plane, 1, 0))
        return up, down

    def tendency(plane, above, below, up, down, rate, forcing):
        beside = above + below + up + down
        beside = beside + pltpu.roll(plane, 1, 1) + pltpu.roll(plane, cells_z - 1, 1)
        return rate * (beside - 6.0 * plane) + forcing

    low1, high1 = grp_layer(0)
    low2, high2 = grp_layer(1)
    low_rate, high_rate = grp_layer(2)
    low_force, high_force = grp_layer(3)
    left1, right1 = slab_layer(0)
    left2, right2 = slab_layer(1)
    left_rate, right_rate = slab_layer(2)
    left_force, right_force = slab_layer(3)
    low_left, low_right = corner(0)
    high_left, high_right = corner(1)

    planes = [low2, low1] + [v_ref[i] for i in range(cells_x)] + [high1, high2]
    rates = [low_rate] + [rate_ref[i] for i in range(cells_x)] + [high_rate]
    forces = [low_force] + [forcing_ref[i] for i in range(cells_x)] + [high_force]
    lefts = [low_left] + [left1[i : i + 1] for i in range(cells_x)] + [high_left]
    rights = [low_right] + [right1[i : i + 1] for i in range(cells_x)] + [high_right]
    stepped = []
    for i in range(cells_x + 2):
        plane = planes[i + 1]
        up, down = shifted(plane, lefts[i], rights[i])
        stepped.append(plane + tendency(plane, planes[i + 2], planes[i], up, down, rates[i], forces[i]))

    def column_step(near, far, inner, rate, forcing, low, high):
        above, below = shifted(near, low, high)
        return near + tendency(near, above, below, inner, far, rate, forcing)

    left_inner = v_ref[:, 0, :]
    right_inner = v_ref[:, cells_y - 1, :]
    left_new = column_step(left1, left2, left_inner, left_rate, left_force, low_left, high_left)
    right_new = column_step(right1, right2, right_inner, right_rate, right_force, low_right, high_right)
    for i in range(cells_x):
        plane = stepped[i + 1]
        up, down = shifted(plane, left_new[i : i + 1], right_new[i : i + 1])
        moved = tendency(plane, stepped[i + 2], stepped[i], up, down, rate_ref[i], forcing_ref[i])
        previous[8 * i : 8 * i + 8, 0:cells_z] = plane
        change[8 * i : 8 * i + 8, 0:cells_z] = moved
    count = line_ref.shape[0]
    previous[:, cells_z : cells_z + LANES] = jnp.zeros((8 * cells_x, LANES), jnp.float32)
    change[:, cells_z : cells_z + LANES] = jnp.zeros((8 * cells_x, LANES), jnp.float32)
    for move in moves:
        move.wait()
    for t in range(count):
        line, start = line_ref[t], start_ref[t]
        base = pl.multiple_of((start // LANES) * LANES, LANES)
        turn = lax.rem(2 * LANES - lax.rem(start, LANES), 2 * LANES)
        row = previous[pl.ds(line, 1), pl.ds(base, 2 * LANES)]
        inputs_ref[t : t + 1, :] = pltpu.roll(row, turn, 1)[:, :SUB]
        row = change[pl.ds(line, 1), pl.ds(base, 2 * LANES)]
        targets_ref[t : t + 1, :] = pltpu.roll(row, turn, 1)[:, :SUB]

    table = table_ref[...]
    cos_w, sin_w = table[2 * MODES : 3 * MODES], table[3 * MODES :]
    inputs = inputs_ref[...]
    waves = lax.dot_general(
        table[: 2 * MODES], inputs, NT, precision=HIGHEST, preferred_element_type=jnp.float32
    )
    tail = lax.broadcasted_iota(jnp.int32, (8, SUB), 0)
    projection = projection_ref[...]
    channel_map = map_ref[...]
    held = jnp.zeros((width, SUB), jnp.float32)
    lane = lax.broadcasted_iota(jnp.int32, (1, LANES), 1)
    losses = jnp.zeros((1, LANES), jnp.float32)
    root = math.sqrt(2.0 / math.pi)
    for t in range(count):
        real, imag = waves[:MODES, t : t + 1], waves[MODES:, t : t + 1]
        line = inputs_ref[t : t + 1, :]
        rest = jnp.where(tail == 0, line, jnp.where(tail == 1, 1.0, 0.0))
        feature = jnp.concatenate([real * cos_w + imag * sin_w, imag * cos_w - real * sin_w, rest], axis=0)
        coarse = feature.astype(jnp.bfloat16).astype(jnp.float32)
        fine = feature - coarse
        zeros = jnp.zeros((LANES - 3 * FEATURES, SUB), jnp.float32)
        stack = jnp.concatenate([coarse, fine, coarse, zeros], axis=0).astype(jnp.bfloat16)
        feature_ref[:, t * SUB : (t + 1) * SUB] = stack
        before = jnp.dot(channel_map, stack, preferred_element_type=jnp.float32)
        square = before * before
        bend = jnp.tanh(root * (before + 0.044715 * (before * square)))
        half = 0.5 * (1.0 + bend)
        after = before * half
        slope = half + (0.5 * root) * before * (1.0 - bend * bend) * (1.0 + (3 * 0.044715) * square)
        output = jnp.sum(after * projection, axis=0, keepdims=True)
        differ = output - targets_ref[t : t + 1, :]
        error = jnp.sum(differ * differ, axis=1, keepdims=True)
        losses = losses + jnp.where(lane == assign_ref[t], error, 0.0)
        pull = (2.0 * scale) * differ
        held = held + after * pull
        slope = slope * projection * pull
        coarse = slope.astype(jnp.bfloat16).astype(jnp.float32)
        slope_ref[0:width, t * SUB : (t + 1) * SUB] = coarse.astype(jnp.bfloat16)
        slope_ref[width : 2 * width, t * SUB : (t + 1) * SUB] = (slope - coarse).astype(jnp.bfloat16)
    pairs = lax.dot_general(
        feature_ref[...], slope_ref[...], NT, preferred_element_type=jnp.float32
    )
    total = pairs[0:FEATURES, 0:width] + pairs[FEATURES : 2 * FEATURES, 0:width] + pairs[0:FEATURES, width:]
    pay_ref[...] = jnp.zeros_like(pay_ref)
    pay_ref[0:MODES, :] = jnp.concatenate([total[0:MODES], total[MODES : 2 * MODES]], axis=1)
    row = 2 * MODES
    pay_ref[MODES : MODES + 1, :] = jnp.concatenate([total[row : row + 1], total[row + 1 : row + 2]], axis=1)
    ones = jnp.ones((8, SUB), jnp.float32)
    summed = lax.dot_general(ones, held, NT, precision=HIGHEST, preferred_element_type=jnp.float32)
    pay_ref[MODES + 1 : MODES + 2, 0:width] = summed[0:1]
    pay_ref[pl.ds(MODES + 2 + lax.axis_index("grp"), 1), :] = losses


def field_kernel(previous, change, _, out_ref):
    cells_x, _, cells_z = out_ref.shape
    for i in range(cells_x):
        at = slice(8 * i, 8 * i + 8)
        out_ref[i] = previous[at, 0:cells_z] + change[at, 0:cells_z]


def base_kernel(masks, width, spectral_ref, mine_ref, other_ref, out_ref):
    here = lax.axis_index("grp") * lax.axis_size("slab") + lax.axis_index("slab")
    even = lax.rem(here, 2) == 0
    rows = width // 2
    low = lax.broadcasted_iota(jnp.int32, (rows, LANES), 1) < width
    for number in range(mine_ref.shape[0] // rows):
        source = here
        for bit, mask in enumerate(masks):
            if number >> bit & 1:
                source = source ^ mask
        columns = pl.ds(pl.multiple_of((source // 2) * LANES, LANES), LANES)
        mine = mine_ref[number * rows : (number + 1) * rows, :]
        other = other_ref[number * rows : (number + 1) * rows, :]
        first, second = jnp.where(even, mine, other), jnp.where(even, other, mine)
        top = jnp.where(low, first, pltpu.roll(second, width, 1))
        bottom = jnp.where(low, pltpu.roll(first, width, 1), second)
        factor = learn_rate * decay_rate
        out_ref[0:rows, columns] = spectral_ref[0:rows, columns] - factor * top
        out_ref[rows : 2 * rows, columns] = spectral_ref[rows : 2 * rows, columns] - factor * bottom


def update_kernel(
    width, lines, groups, pay_ref, spectral_ref, base_ref, dense_ref, momentum_ref, row_ref,
    spectral_hbm, dense_out, momentum_out, loss_out, square, result, sems,
):
    first, second = lax.axis_index("grp"), lax.axis_index("slab")
    here = first * lax.axis_size("slab") + second
    square[...] = jnp.zeros_like(square)
    square[0:MODES, 0:width] = pay_ref[0:MODES, 0:width]
    square[MODES : 2 * MODES, 0:width] = pay_ref[0:MODES, width : 2 * width]
    slopes = pay_ref[MODES : MODES + 2, :]
    square[2 * MODES : 2 * MODES + 1, 0:width] = slopes[0:1, 0:width]
    square[2 * MODES + 1 : 2 * MODES + 2, 0:width] = slopes[0:1, width : 2 * width]
    square[2 * MODES + 2 : 2 * MODES + 3, 0:width] = slopes[1:2, 0:width]
    turned = square[...].T[0:width, :]
    gains, biases = row_ref[0:1, :], row_ref[1:2, :]
    by_input = turned[:, 2 * MODES : 2 * MODES + 1]
    by_one = turned[:, 2 * MODES + 1 : 2 * MODES + 2]
    by_output = turned[:, 2 * MODES + 2 : 2 * MODES + 3]
    lane = lax.broadcasted_iota(jnp.int32, (width, LANES), 1)
    low = lane < width
    gathered = jnp.zeros((width, LANES), jnp.float32)
    copies = []
    for pair in range(MODES):
        span = slice(pair * LANES, (pair + 1) * LANES)
        column = jnp.where(low, turned[:, 2 * pair : 2 * pair + 1], turned[:, 2 * pair + 1 : 2 * pair + 2])
        gradient = gains * column
        if pair == 0:
            gradient = gradient + jnp.where(low, biases * by_one, 0.0)
        result[:, span] = base_ref[:, span] - learn_rate * gradient
        gathered = gathered + spectral_ref[:, span] * column
        if (pair + 1) % (MODES // groups) == 0:
            number = len(copies)
            part = pl.ds(number * (MODES // groups) * LANES, (MODES // groups) * LANES)
            copies.append(pltpu.make_async_copy(result.at[:, part], spectral_hbm.at[:, part], sems.at[number]))
            copies[-1].start()
    mixing = dense_ref[:, 0:width]
    gain_row = jnp.sum(gathered, axis=0, keepdims=True)
    gain_row = gain_row[:, 0:width] + gain_row[:, width:] + jnp.sum(mixing * by_input, axis=0, keepdims=True)
    bias_row = jnp.sum((mixing + spectral_ref[:, 0:width]) * by_one, axis=0, keepdims=True)
    dense_out[:, 0:width] = mixing - dense_rate * (gains[:, 0:width] * by_input + biases[:, 0:width] * by_one)
    tail = dense_ref[:, width : width + 4]
    lane4 = lax.broadcasted_iota(jnp.int32, (width, 4), 1)
    change = jnp.where(
        lane4 == 0, as_column(gain_row), jnp.where(
            lane4 == 1, as_column(bias_row), jnp.where(lane4 == 2, by_one, by_output)))
    dense_out[:, width : width + 4] = tail - dense_rate * change
    piece = momentum_ref.shape[0]
    block = here * piece // width
    inside = here * piece - block * width
    square[0 : width, :] = jnp.where(low, dense_ref[:, width : width + 1], dense_ref[:, width + 1 : width + 2])
    at = pl.ds(0 if piece == width else pl.multiple_of(inside, piece), piece)
    half = block // MODES
    mode = block - half * MODES
    row = pay_ref[pl.ds(mode, 1), :]
    row = jnp.where(half == 0, row[:, 0:width], row[:, width : 2 * width])
    gradient = square[at, 0:1] * row
    gradient = gradient + jnp.where(block == 0, square[at, width : width + 1] * slopes[0:1, width : 2 * width], 0.0)
    momentum_out[...] = decay_rate * momentum_ref[...] + gradient
    sums = pay_ref[pl.ds(MODES + 2 + first, 1), :]
    lane = lax.broadcasted_iota(jnp.int32, (1, LANES), 1)
    own = jnp.sum(jnp.where(lane == second, sums, 0.0), axis=1, keepdims=True)
    loss_out[...] = own * (1.0 / (lines * SUB))
    for copy in copies:
        copy.wait()


def hop_masks(n_grp, n_slab):
    masks, bit = [], 0
    while 1 << bit < n_slab:
        masks.append(3 << (bit - 1) if bit > 2 and bit % 2 else 1 << bit)
        bit += 1
    bit = 1
    while bit < n_grp:
        masks.append(bit * n_slab)
        bit *= 2
    return masks


def in_hbm(array):
    return pltpu.with_memory_space_constraint(array, pltpu.HBM)


def swap(array, mask, count):
    return lax.ppermute(array, AXES, [(i, i ^ mask) for i in range(count)])


def local(velocity, rate, forcing, anchor_line, anchor_z, assign, spectral, dense, momentum):
    n_grp, n_slab = lax.axis_size("grp"), lax.axis_size("slab")
    devices = n_grp * n_slab
    width = dense.shape[1]
    lines = anchor_line.shape[0]
    cells_x, _, cells_z = velocity.shape
    chunks = cells_z // LANES
    halo_rows = 4 * 8 * chunks
    piece = momentum.shape[0]
    packed = piece // 2
    f32 = jnp.float32
    joined = n_grp == 2 and piece == width and devices & (devices - 1) == 0
    two_sided = n_grp != 2
    table = jnp.asarray(tables())
    spectral, dense = spectral.T, dense.T

    edge_rows = halo_rows + (packed if joined else 0)
    velocity, rate, forcing, near_momentum, *edges = call(
        functools.partial(edge_kernel, joined),
        [(velocity.shape, f32)] * 3 + [(momentum.shape, f32)]
        + [((edge_rows, LANES), f32)] * (2 if two_sided else 1),
        scratch=[pltpu.SemaphoreType.DMA((4,))],
        ins=[HBM] * 4,
    )(*(in_hbm(array) for array in (velocity, rate, forcing, momentum)))
    if two_sided:
        low = lax.ppermute(edges[0], "grp", [(i, i + 1) for i in range(n_grp - 1)])
        high = lax.ppermute(edges[1], "grp", [(i + 1, i) for i in range(n_grp - 1)])
    else:
        low = high = lax.ppermute(edges[0], "grp", [(0, 1), (1, 0)])
    message = (halo_rows + 2 * chunks, LANES)
    outs = [(message, f32), (message, f32)] + ([((2 * packed, LANES), f32)] if joined else [])
    to_a, to_b, *gathered = call(
        functools.partial(side_kernel, two_sided, packed if joined else 0), outs, ins=[VMEM] * 6
    )(velocity, rate, forcing, low, high, edges[0])
    pairs = [(i, i ^ 1) for i in range(n_slab)]
    odd = [(i, i + 1) for i in range(1, n_slab - 1, 2)]
    from_b = lax.ppermute(to_b, "slab", odd + [(j, i) for i, j in odd])
    from_a = lax.ppermute(to_a, "slab", pairs)
    channel_map, projection, rows = call(
        functools.partial(feature_kernel, width),
        [((width, LANES), jnp.bfloat16), ((width, LANES), f32), ((8, LANES), f32)],
        ins=[VMEM] * 2,
    )(spectral, dense)
    pay_rows = -(-(MODES + 2 + n_grp) // 8) * 8
    scale = 1.0 / (devices * lines * SUB)
    window = ((8 * cells_x, cells_z + LANES), f32)
    previous, change, payload = call(
        functools.partial(step_kernel, two_sided, width, scale),
        [window, window, ((pay_rows, LANES), f32)],
        scratch=[pltpu.SMEM((lines,), jnp.int32)] * 3 + [
            pltpu.SemaphoreType.DMA((3,)),
            pltpu.VMEM((lines, SUB), f32),
            pltpu.VMEM((lines, SUB), f32),
            pltpu.VMEM((LANES, lines * SUB), jnp.bfloat16),
            pltpu.VMEM((2 * width, lines * SUB), jnp.bfloat16),
        ],
        ins=[VMEM] * 7 + [HBM] * 3 + [VMEM] * 3,
    )(velocity, rate, forcing, low, high, from_a, from_b,
      in_hbm(anchor_line), in_hbm(anchor_z), in_hbm(assign.reshape(-1)), channel_map, projection, table)

    masks = hop_masks(n_grp, n_slab)
    if joined:
        mine = gathered[0]
        order = [n_slab] + [m for m in masks if m not in (1, n_slab)] + [1]
        for mask in order[1:-1]:
            other = swap(mine, mask, devices)
            mine = jnp.concatenate([mine, other], axis=0)
        other = swap(mine, order[-1], devices)
        base = call(
            functools.partial(base_kernel, order[:-1], width), [(spectral.shape, f32)], ins=[VMEM] * 3
        )(spectral, mine, other)[0]
        masks = [1, n_slab] + [m for m in masks if m not in (1, n_slab)]
    else:
        whole = lax.all_gather(momentum, AXES, axis=0, tiled=True)
        base = spectral - (learn_rate * decay_rate) * whole.T
    anchor = payload
    if devices & (devices - 1) == 0:
        for number, mask in enumerate(masks):
            payload = payload + swap(payload, mask, devices)
            if number == 0:
                anchor = payload
    else:
        payload = lax.psum(payload, AXES)
    field_now = call(field_kernel, [(velocity.shape, f32)], ins=[VMEM, VMEM, HBM])(previous, change, anchor)[0]
    groups = 4
    spectral_new, dense_new, momentum_new, trainer_loss = call(
        functools.partial(update_kernel, width, lines, groups),
        [(spectral.shape, f32), (dense.shape, f32), (momentum.shape, f32), ((1, 1), f32)],
        scratch=[pltpu.VMEM((LANES, LANES), f32), pltpu.VMEM(spectral.shape, f32), pltpu.SemaphoreType.DMA((groups,))],
        ins=[VMEM] * 6,
        places=[HBM, VMEM, VMEM, VMEM],
    )(payload, spectral, base, dense, near_momentum, rows)
    return (field_now, trainer_loss, spectral_new.T, dense_new.T, momentum_new)


def solution(mesh):
    placed = (
        P("grp", "slab", None),
        P("grp", "slab", None),
        P("grp", "slab", None),
        P(("grp", "slab")),
        P(("grp", "slab")),
        P(("grp", "slab"), None),
        P(),
        P(),
        P(("grp", "slab"), None),
    )

    return jax.shard_map(
        local,
        mesh=mesh,
        in_specs=placed,
        out_specs=(P("grp", "slab", None), P("grp", "slab"), P(), P(), P(("grp", "slab"), None)),
        check_vma=False,
    )
```

```python
import functools
import math

import jax
import jax.numpy as jnp
import numpy as np
from jax import lax
from jax.experimental import pallas as pl
from jax.experimental.pallas import tpu as pltpu
from jax.sharding import PartitionSpec as P


SUB = 128
MODES = 16
LANES = 128
FEATURES = 2 * MODES + 8

decay_rate = 0.9
learn_rate = 0.5
dense_rate = 3.0

AXES = ("grp", "slab")
HIGHEST = lax.Precision.HIGHEST
NT = (((1,), (1,)), ((), ()))
VMEM = pl.BlockSpec(memory_space=pltpu.VMEM)
HBM = pl.BlockSpec(memory_space=pltpu.HBM)


def call(kernel, outs, scratch=(), ins=(), places=None, flops=1000000):
    outs = [jax.ShapeDtypeStruct(shape, dtype) for shape, dtype in outs]
    size = sum(math.prod(o.shape) * o.dtype.itemsize for o in outs)
    return pl.pallas_call(
        kernel,
        out_shape=outs,
        in_specs=list(ins),
        out_specs=places or [VMEM] * len(outs),
        scratch_shapes=list(scratch),
        compiler_params=pltpu.CompilerParams(vmem_limit_bytes=16 << 20),
        cost_estimate=pl.CostEstimate(flops=flops, bytes_accessed=2 * size, transcendentals=0),
    )


def tables():
    counts = np.arange(SUB)
    waves = np.arange(MODES)
    angle = (waves[:, None] * counts[None, :] % SUB) * (2.0 * np.pi / SUB)
    weight = np.where(waves == 0, 1.0, 2.0)[:, None] / SUB
    cosine, sine = np.cos(angle), np.sin(angle)
    return np.concatenate([cosine, sine, weight * cosine, weight * sine]).astype(np.float32)


def put_plane(ref, row, plane):
    for q in range(plane.shape[1] // LANES):
        ref[row + 8 * q : row + 8 * q + 8, :] = plane[:, q * LANES : (q + 1) * LANES]


def get_plane(ref, row, chunks):
    return jnp.concatenate([ref[row + 8 * q : row + 8 * q + 8, :] for q in range(chunks)], axis=1)


def pack_rows(block):
    half = block.shape[0] // 2
    return jnp.concatenate([block[:half], block[half:]], axis=1)


LAYERS = 3


def beside_in_z(plane):
    size = plane.shape[1]
    return pltpu.roll(plane, 1, 1) + pltpu.roll(plane, size - 1, 1)


def shifted(plane, before, after):
    sublane = lax.broadcasted_iota(jnp.int32, plane.shape, 0)
    last = plane.shape[0] - 1
    up = jnp.where(sublane == last, after, pltpu.roll(plane, last, 0))
    down = jnp.where(sublane == 0, before, pltpu.roll(plane, 1, 0))
    return up, down


def edge_kernel(with_momentum, sides, v_hbm, rate_hbm, forcing_hbm, momentum_hbm, *rest):
    momentum_ref, planes, momentum_scratch, sems = rest[sides], *rest[-3:]
    last = v_hbm.shape[0] - 1
    chunks = v_hbm.shape[2] // LANES
    moves = []

    def move(source, target):
        moves.append(pltpu.make_async_copy(source, target, sems.at[len(moves)]))
        moves[-1].start()

    highs = [lax.axis_index("grp") == 0] if sides == 1 else [True, False]
    move(momentum_hbm, momentum_scratch)
    for number, high in enumerate(highs):
        edge = jnp.where(high, last, 0)
        second = jnp.where(high, last - 1, 1)
        for layer, (ref, at) in enumerate(((v_hbm, edge), (v_hbm, second), (rate_hbm, edge), (forcing_hbm, edge))):
            move(ref.at[at], planes.at[4 * number + layer])
    moves[0].wait()
    block = momentum_scratch[...]
    momentum_ref[...] = block
    if with_momentum:
        packed = pack_rows(block.T)
        start = LAYERS * 8 * chunks
        rest[0][start : start + packed.shape[0], :] = packed
    for item in moves[1:]:
        item.wait()
    for number in range(sides):
        edge, second, rate, forcing = (planes[4 * number + layer] for layer in range(4))
        up, down = shifted(edge, 0.0, 0.0)
        partial = edge + (rate * (second + up + down + beside_in_z(edge) - 6.0 * edge) + forcing)
        for layer, plane in enumerate((edge, rate, partial)):
            put_plane(rest[number], layer * 8 * chunks, plane)


def stage_kernel(v_hbm, rate_hbm, forcing_hbm, v_ref, rate_ref, forcing_ref, sems):
    pairs = ((v_hbm, v_ref), (rate_hbm, rate_ref), (forcing_hbm, forcing_ref))
    moves = [pltpu.make_async_copy(*pair, sems.at[number]) for number, pair in enumerate(pairs)]
    for move in moves:
        move.start()
    for move in moves:
        move.wait()


def grp_halo(two_sided, ref_low, ref_high, layer, chunks):
    rows = 8 * chunks * layer
    if two_sided:
        return get_plane(ref_low, rows, chunks), get_plane(ref_high, rows, chunks)
    plane = get_plane(ref_low, rows, chunks)
    first = lax.axis_index("grp") == 0
    return jnp.where(first, 0.0, plane), jnp.where(first, plane, 0.0)


def side_kernel(two_sided, packed_rows, v_ref, rate_ref, forcing_ref, low_ref, high_ref, own_ref, *outs):
    a_ref, b_ref = outs[:2]
    last = v_ref.shape[1] - 1
    chunks = v_ref.shape[2] // LANES
    even = lax.rem(lax.axis_index("slab"), 2) == 0
    low, high = grp_halo(two_sided, low_ref, high_ref, 0, chunks)
    messages = []
    for at, inside in ((0, 1), (last, last - 1)):
        edge, second, rate = v_ref[:, at, :], v_ref[:, inside, :], rate_ref[:, at, :]
        below, above = low[at : at + 1], high[at : at + 1]
        up, down = shifted(edge, below, above)
        beside = up + down + second + beside_in_z(edge)
        partial = edge + (rate * (beside - 6.0 * edge) + forcing_ref[:, at, :])
        messages.append((edge, rate, partial, below, above))
    start = LAYERS * 8 * chunks
    for number, (left, right) in enumerate(zip(*messages)):
        for ref, plane in ((a_ref, jnp.where(even, right, left)), (b_ref, jnp.where(even, left, right))):
            if number < LAYERS:
                put_plane(ref, number * 8 * chunks, plane)
                continue
            for q in range(chunks):
                row = start + (number - LAYERS) * chunks + q
                ref[row : row + 1, :] = plane[:, q * LANES : (q + 1) * LANES]
    if packed_rows:
        outs[2][0:packed_rows, :] = own_ref[start : start + packed_rows, :]
        outs[2][packed_rows : 2 * packed_rows, :] = low_ref[start : start + packed_rows, :]


def as_row(column):
    size = column.shape[0]
    square = (size, size)
    same = lax.broadcasted_iota(jnp.int32, square, 0) == lax.broadcasted_iota(jnp.int32, square, 1)
    return jnp.sum(jnp.where(same, column, 0.0), axis=0, keepdims=True)


def as_column(row):
    size = row.shape[1]
    square = (size, size)
    same = lax.broadcasted_iota(jnp.int32, square, 0) == lax.broadcasted_iota(jnp.int32, square, 1)
    return jnp.sum(jnp.where(same, row, 0.0), axis=1, keepdims=True)


def feature_kernel(width, spectral_ref, dense_ref, map_ref, projection_ref, row_ref):
    gain = as_row(dense_ref[:, width : width + 1])
    bias = as_row(dense_ref[:, width + 1 : width + 2])
    projection_ref[...] = jnp.broadcast_to(dense_ref[:, width + 3 : width + 4], (width, LANES))
    row_ref[...] = jnp.zeros_like(row_ref)
    row_ref[0:1, :] = jnp.concatenate([gain, gain], axis=1)
    row_ref[1:2, :] = jnp.concatenate([bias, bias], axis=1)
    gains = row_ref[0:1, :]
    lane = lax.broadcasted_iota(jnp.int32, (width, LANES), 1)
    low = lane < width
    full = jnp.zeros((width, LANES), jnp.float32)
    for pair in range(MODES):
        product = spectral_ref[:, pair * LANES : (pair + 1) * LANES] * gains
        first = jnp.sum(jnp.where(low, product, 0.0), axis=1, keepdims=True)
        second = jnp.sum(jnp.where(low, 0.0, product), axis=1, keepdims=True)
        full = jnp.where(lane == 2 * pair, first, jnp.where(lane == 2 * pair + 1, second, full))
    mixing = dense_ref[:, 0:width]
    by_input = jnp.sum(gain * mixing, axis=1, keepdims=True)
    by_one = jnp.sum(bias * (mixing + spectral_ref[:, 0:width]), axis=1, keepdims=True)
    by_one = by_one + dense_ref[:, width + 2 : width + 3]
    full = jnp.where(lane == 2 * MODES, by_input, jnp.where(lane == 2 * MODES + 1, by_one, full))
    coarse = full.astype(jnp.bfloat16).astype(jnp.float32)
    fine = full - coarse
    joined = coarse + pltpu.roll(coarse, FEATURES, 1) + pltpu.roll(fine, 2 * FEATURES, 1)
    map_ref[...] = joined.astype(jnp.bfloat16)


def step_kernel(
    two_sided, width, scale, v_ref, rate_ref, forcing_ref, low_ref, high_ref, a_ref, b_ref,
    line_hbm, start_hbm, assign_hbm, map_ref, projection_ref, table_ref,
    previous, change, pay_ref, line_ref, start_ref, assign_ref, sems,
    inputs_ref, targets_ref, feature_ref, slope_ref,
):
    moves = [
        pltpu.make_async_copy(source, target, sems.at[number])
        for number, (source, target) in enumerate(
            ((line_hbm, line_ref), (start_hbm, start_ref), (assign_hbm, assign_ref))
        )
    ]
    for move in moves:
        move.start()
    cells_x, cells_y, cells_z = v_ref.shape
    chunks = cells_z // LANES
    slab = lax.axis_index("slab")
    even = lax.rem(slab, 2) == 0
    inner = jnp.logical_and(slab > 0, slab < lax.axis_size("slab") - 1)

    def grp_layer(layer):
        return grp_halo(two_sided, low_ref, high_ref, layer, chunks)

    def slab_layer(layer):
        from_a = get_plane(a_ref, 8 * chunks * layer, chunks)
        from_b = jnp.where(inner, get_plane(b_ref, 8 * chunks * layer, chunks), 0.0)
        return jnp.where(even, from_b, from_a), jnp.where(even, from_a, from_b)

    def corner(number):
        start = LAYERS * 8 * chunks + number * chunks
        from_a = jnp.concatenate([a_ref[start + q : start + q + 1, :] for q in range(chunks)], axis=1)
        from_b = jnp.concatenate([b_ref[start + q : start + q + 1, :] for q in range(chunks)], axis=1)
        from_b = jnp.where(inner, from_b, 0.0)
        return jnp.where(even, from_b, from_a), jnp.where(even, from_a, from_b)

    def tendency(plane, above, below, up, down, rate, forcing):
        beside = above + below + up + down + beside_in_z(plane)
        return rate * (beside - 6.0 * plane) + forcing

    low, high = grp_layer(0)
    low_rate, high_rate = grp_layer(1)
    low_part, high_part = grp_layer(2)
    left, right = slab_layer(0)
    left_rate, right_rate = slab_layer(1)
    left_part, right_part = slab_layer(2)
    sublane = lax.broadcasted_iota(jnp.int32, (cells_y, cells_z), 0)

    def halo_step(part, rate, inner, corners):
        at_ends = jnp.where(sublane == 0, corners[0], jnp.where(sublane == cells_y - 1, corners[1], 0.0))
        return part + rate * (inner + at_ends)

    planes = [low] + [v_ref[i] for i in range(cells_x)] + [high]
    stepped = [halo_step(low_part, low_rate, planes[1], corner(0))]
    for i in range(cells_x):
        plane = planes[i + 1]
        up, down = shifted(plane, left[i : i + 1], right[i : i + 1])
        stepped.append(plane + tendency(plane, planes[i + 2], planes[i], up, down, rate_ref[i], forcing_ref[i]))
    stepped.append(halo_step(high_part, high_rate, planes[cells_x], corner(1)))
    left_new = left_part + left_rate * v_ref[:, 0, :]
    right_new = right_part + right_rate * v_ref[:, cells_y - 1, :]
    for i in range(cells_x):
        plane = stepped[i + 1]
        up, down = shifted(plane, left_new[i : i + 1], right_new[i : i + 1])
        moved = tendency(plane, stepped[i + 2], stepped[i], up, down, rate_ref[i], forcing_ref[i])
        previous[8 * i : 8 * i + 8, 0:cells_z] = plane
        change[8 * i : 8 * i + 8, 0:cells_z] = moved
    count = line_ref.shape[0]
    previous[:, cells_z : cells_z + LANES] = jnp.zeros((8 * cells_x, LANES), jnp.float32)
    change[:, cells_z : cells_z + LANES] = jnp.zeros((8 * cells_x, LANES), jnp.float32)
    for move in moves:
        move.wait()
    for t in range(count):
        line, start = line_ref[t], start_ref[t]
        base = pl.multiple_of((start // LANES) * LANES, LANES)
        turn = lax.rem(2 * LANES - lax.rem(start, LANES), 2 * LANES)
        row = previous[pl.ds(line, 1), pl.ds(base, 2 * LANES)]
        inputs_ref[t : t + 1, :] = pltpu.roll(row, turn, 1)[:, :SUB]
        row = change[pl.ds(line, 1), pl.ds(base, 2 * LANES)]
        targets_ref[t : t + 1, :] = pltpu.roll(row, turn, 1)[:, :SUB]

    table = table_ref[...]
    cos_w, sin_w = table[2 * MODES : 3 * MODES], table[3 * MODES :]
    inputs = inputs_ref[...]
    waves = lax.dot_general(
        table[: 2 * MODES], inputs, NT, precision=HIGHEST, preferred_element_type=jnp.float32
    )
    tail = lax.broadcasted_iota(jnp.int32, (8, SUB), 0)
    projection = projection_ref[...]
    channel_map = map_ref[...]
    held = jnp.zeros((width, SUB), jnp.float32)
    lane = lax.broadcasted_iota(jnp.int32, (1, LANES), 1)
    losses = jnp.zeros((1, LANES), jnp.float32)
    root = math.sqrt(2.0 / math.pi)
    for t in range(count):
        real, imag = waves[:MODES, t : t + 1], waves[MODES:, t : t + 1]
        line = inputs_ref[t : t + 1, :]
        rest = jnp.where(tail == 0, line, jnp.where(tail == 1, 1.0, 0.0))
        feature = jnp.concatenate([real * cos_w + imag * sin_w, imag * cos_w - real * sin_w, rest], axis=0)
        coarse = feature.astype(jnp.bfloat16).astype(jnp.float32)
        fine = feature - coarse
        zeros = jnp.zeros((LANES - 3 * FEATURES, SUB), jnp.float32)
        stack = jnp.concatenate([coarse, fine, coarse, zeros], axis=0).astype(jnp.bfloat16)
        feature_ref[:, t * SUB : (t + 1) * SUB] = stack
        before = jnp.dot(channel_map, stack, preferred_element_type=jnp.float32)
        square = before * before
        bend = jnp.tanh(root * (before + 0.044715 * (before * square)))
        half = 0.5 * (1.0 + bend)
        after = before * half
        slope = half + (0.5 * root) * before * (1.0 - bend * bend) * (1.0 + (3 * 0.044715) * square)
        output = jnp.sum(after * projection, axis=0, keepdims=True)
        differ = output - targets_ref[t : t + 1, :]
        error = jnp.sum(differ * differ, axis=1, keepdims=True)
        losses = losses + jnp.where(lane == assign_ref[t], error, 0.0)
        pull = (2.0 * scale) * differ
        held = held + after * pull
        slope = slope * projection * pull
        coarse = slope.astype(jnp.bfloat16).astype(jnp.float32)
        slope_ref[0:width, t * SUB : (t + 1) * SUB] = coarse.astype(jnp.bfloat16)
        slope_ref[width : 2 * width, t * SUB : (t + 1) * SUB] = (slope - coarse).astype(jnp.bfloat16)
    pairs = lax.dot_general(
        feature_ref[...], slope_ref[...], NT, preferred_element_type=jnp.float32
    )
    total = pairs[0:FEATURES, 0:width] + pairs[FEATURES : 2 * FEATURES, 0:width] + pairs[0:FEATURES, width:]
    pay_ref[...] = jnp.zeros_like(pay_ref)
    pay_ref[0:MODES, :] = jnp.concatenate([total[0:MODES], total[MODES : 2 * MODES]], axis=1)
    row = 2 * MODES
    pay_ref[MODES : MODES + 1, :] = jnp.concatenate([total[row : row + 1], total[row + 1 : row + 2]], axis=1)
    ones = jnp.ones((8, SUB), jnp.float32)
    summed = lax.dot_general(ones, held, NT, precision=HIGHEST, preferred_element_type=jnp.float32)
    pay_ref[MODES + 1 : MODES + 2, 0:width] = summed[0:1]
    pay_ref[pl.ds(MODES + 2 + lax.axis_index("grp"), 1), :] = losses


def field_kernel(previous, change, _, out_ref):
    cells_x, _, cells_z = out_ref.shape
    for i in range(cells_x):
        at = slice(8 * i, 8 * i + 8)
        out_ref[i] = previous[at, 0:cells_z] + change[at, 0:cells_z]


def base_kernel(masks, width, spectral_ref, mine_ref, other_ref, out_ref):
    here = lax.axis_index("grp") * lax.axis_size("slab") + lax.axis_index("slab")
    rows = width // 2
    low = lax.broadcasted_iota(jnp.int32, (rows, LANES), 1) < width
    for number in range(mine_ref.shape[0] // rows):
        source = here
        for bit, mask in enumerate(masks):
            if number >> bit & 1:
                source = source ^ mask
        even = lax.rem(source, 2) == 0
        columns = pl.ds(pl.multiple_of((source // 2) * LANES, LANES), LANES)
        mine = mine_ref[number * rows : (number + 1) * rows, :]
        other = other_ref[number * rows : (number + 1) * rows, :]
        first, second = jnp.where(even, mine, other), jnp.where(even, other, mine)
        top = jnp.where(low, first, pltpu.roll(second, width, 1))
        bottom = jnp.where(low, pltpu.roll(first, width, 1), second)
        factor = learn_rate * decay_rate
        out_ref[0:rows, columns] = spectral_ref[0:rows, columns] - factor * top
        out_ref[rows : 2 * rows, columns] = spectral_ref[rows : 2 * rows, columns] - factor * bottom


def update_kernel(
    width, lines, groups, pay_ref, spectral_ref, base_ref, dense_ref, momentum_ref, row_ref,
    spectral_hbm, dense_hbm, momentum_hbm, loss_hbm, square, result, dense_out, momentum_out, loss_out, sems,
):
    first, second = lax.axis_index("grp"), lax.axis_index("slab")
    here = first * lax.axis_size("slab") + second
    square[...] = jnp.zeros_like(square)
    square[0:MODES, 0:width] = pay_ref[0:MODES, 0:width]
    square[MODES : 2 * MODES, 0:width] = pay_ref[0:MODES, width : 2 * width]
    slopes = pay_ref[MODES : MODES + 2, :]
    square[2 * MODES : 2 * MODES + 1, 0:width] = slopes[0:1, 0:width]
    square[2 * MODES + 1 : 2 * MODES + 2, 0:width] = slopes[0:1, width : 2 * width]
    square[2 * MODES + 2 : 2 * MODES + 3, 0:width] = slopes[1:2, 0:width]
    turned = square[...].T[0:width, :]
    gains, biases = row_ref[0:1, :], row_ref[1:2, :]
    by_input = turned[:, 2 * MODES : 2 * MODES + 1]
    by_one = turned[:, 2 * MODES + 1 : 2 * MODES + 2]
    by_output = turned[:, 2 * MODES + 2 : 2 * MODES + 3]
    lane = lax.broadcasted_iota(jnp.int32, (width, LANES), 1)
    low = lane < width
    copies = []

    def send(source, target):
        copies.append(pltpu.make_async_copy(source, target, sems.at[len(copies)]))
        copies[-1].start()

    piece = momentum_ref.shape[0]
    block = here * piece // width
    inside = here * piece - block * width
    square[0 : width, :] = jnp.where(low, dense_ref[:, width : width + 1], dense_ref[:, width + 1 : width + 2])
    at = pl.ds(0 if piece == width else pl.multiple_of(inside, piece), piece)
    half = block // MODES
    mode = block - half * MODES
    row = pay_ref[pl.ds(mode, 1), :]
    row = jnp.where(half == 0, row[:, 0:width], row[:, width : 2 * width])
    gradient = square[at, 0:1] * row
    gradient = gradient + jnp.where(block == 0, square[at, width : width + 1] * slopes[0:1, width : 2 * width], 0.0)
    momentum_out[...] = decay_rate * momentum_ref[...] + gradient
    send(momentum_out, momentum_hbm)
    sums = pay_ref[pl.ds(MODES + 2 + first, 1), :]
    lane1 = lax.broadcasted_iota(jnp.int32, (1, LANES), 1)
    own = jnp.sum(jnp.where(lane1 == second, sums, 0.0), axis=1, keepdims=True)
    loss_out[...] = own * (1.0 / (lines * SUB))
    send(loss_out, loss_hbm)
    gathered = jnp.zeros((width, LANES), jnp.float32)
    for pair in range(MODES):
        span = slice(pair * LANES, (pair + 1) * LANES)
        column = jnp.where(low, turned[:, 2 * pair : 2 * pair + 1], turned[:, 2 * pair + 1 : 2 * pair + 2])
        gradient = gains * column
        if pair == 0:
            gradient = gradient + jnp.where(low, biases * by_one, 0.0)
        result[:, span] = base_ref[:, span] - learn_rate * gradient
        gathered = gathered + spectral_ref[:, span] * column
        if (pair + 1) % (MODES // groups) == 0:
            many = (MODES // groups) * LANES
            part = pl.ds((pair + 1) * LANES - many, many)
            send(result.at[:, part], spectral_hbm.at[:, part])
    mixing = dense_ref[:, 0:width]
    gain_row = jnp.sum(gathered, axis=0, keepdims=True)
    gain_row = gain_row[:, 0:width] + gain_row[:, width:] + jnp.sum(mixing * by_input, axis=0, keepdims=True)
    bias_row = jnp.sum((mixing + spectral_ref[:, 0:width]) * by_one, axis=0, keepdims=True)
    dense_out[:, 0:width] = mixing - dense_rate * (gains[:, 0:width] * by_input + biases[:, 0:width] * by_one)
    tail = dense_ref[:, width : width + 4]
    lane4 = lax.broadcasted_iota(jnp.int32, (width, 4), 1)
    change = jnp.where(
        lane4 == 0, as_column(gain_row), jnp.where(
            lane4 == 1, as_column(bias_row), jnp.where(lane4 == 2, by_one, by_output)))
    dense_out[:, width : width + 4] = tail - dense_rate * change
    send(dense_out, dense_hbm)
    for copy in copies:
        copy.wait()


def hop_masks(n_grp, n_slab):
    slab_bits = [1 << bit for bit in range(n_slab.bit_length() - 1)]
    grp_bits = [n_slab << bit for bit in range(n_grp.bit_length() - 1)]
    return [1] + [mask + 1 for mask in grp_bits + slab_bits[1:2] + slab_bits[:1:-1]]


def in_hbm(array):
    return pltpu.with_memory_space_constraint(array, pltpu.HBM)


def swap(array, mask, count):
    return lax.ppermute(array, AXES, [(i, i ^ mask) for i in range(count)])


def local(velocity, rate, forcing, anchor_line, anchor_z, assign, spectral, dense, momentum):
    n_grp, n_slab = lax.axis_size("grp"), lax.axis_size("slab")
    devices = n_grp * n_slab
    width = dense.shape[1]
    lines = anchor_line.shape[0]
    cells_x, cells_y, cells_z = velocity.shape
    chunks = cells_z // LANES
    halo_rows = LAYERS * 8 * chunks
    piece = momentum.shape[0]
    packed = piece // 2
    f32 = jnp.float32
    joined = n_grp == 2 and piece == width and devices & (devices - 1) == 0
    two_sided = n_grp != 2
    table = jnp.asarray(tables())
    spectral, dense = spectral.T, dense.T

    sides = 2 if two_sided else 1
    edge_rows = halo_rows + (packed if joined else 0)
    blocks = [in_hbm(array) for array in (velocity, rate, forcing)]
    *edges, near_momentum = call(
        functools.partial(edge_kernel, joined, sides),
        [((edge_rows, LANES), f32)] * sides + [(momentum.shape, f32)],
        scratch=[
            pltpu.VMEM((4 * sides, cells_y, cells_z), f32),
            pltpu.VMEM(momentum.shape, f32),
            pltpu.SemaphoreType.DMA((1 + 4 * sides,)),
        ],
        ins=[HBM] * 4,
    )(*blocks, in_hbm(momentum))
    velocity, rate, forcing = call(
        stage_kernel, [(velocity.shape, f32)] * 3, scratch=[pltpu.SemaphoreType.DMA((3,))], ins=[HBM] * 3
    )(*blocks)
    if two_sided:
        low = lax.ppermute(edges[0], "grp", [(i, i + 1) for i in range(n_grp - 1)])
        high = lax.ppermute(edges[1], "grp", [(i + 1, i) for i in range(n_grp - 1)])
    else:
        low = high = lax.ppermute(edges[0], "grp", [(0, 1), (1, 0)])
    message = (halo_rows + 2 * chunks, LANES)
    outs = [(message, f32), (message, f32)] + ([((2 * packed, LANES), f32)] if joined else [])
    to_a, to_b, *gathered = call(
        functools.partial(side_kernel, two_sided, packed if joined else 0), outs, ins=[VMEM] * 6
    )(velocity, rate, forcing, low, high, edges[0])
    pairs = [(i, i ^ 1) for i in range(n_slab)]
    odd = [(i, (i + 1) % n_slab) for i in range(1, n_slab, 2)]
    from_b = lax.ppermute(to_b, "slab", odd + [(j, i) for i, j in odd])
    from_a = lax.ppermute(to_a, "slab", pairs)
    channel_map, projection, rows = call(
        functools.partial(feature_kernel, width),
        [((width, LANES), jnp.bfloat16), ((width, LANES), f32), ((8, LANES), f32)],
        ins=[VMEM] * 2,
    )(spectral, dense)
    pay_rows = -(-(MODES + 2 + n_grp) // 8) * 8
    scale = 1.0 / (devices * lines * SUB)
    window = ((8 * cells_x, cells_z + LANES), f32)
    previous, change, payload = call(
        functools.partial(step_kernel, two_sided, width, scale),
        [window, window, ((pay_rows, LANES), f32)],
        scratch=[pltpu.SMEM((lines,), jnp.int32)] * 3 + [
            pltpu.SemaphoreType.DMA((3,)),
            pltpu.VMEM((lines, SUB), f32),
            pltpu.VMEM((lines, SUB), f32),
            pltpu.VMEM((LANES, lines * SUB), jnp.bfloat16),
            pltpu.VMEM((2 * width, lines * SUB), jnp.bfloat16),
        ],
        ins=[VMEM] * 7 + [HBM] * 3 + [VMEM] * 3,
    )(velocity, rate, forcing, low, high, from_a, from_b,
      in_hbm(anchor_line), in_hbm(anchor_z), in_hbm(assign.reshape(-1)), channel_map, projection, table)

    masks = hop_masks(n_grp, n_slab)
    if joined:
        mine = gathered[0]
        order = [n_slab] + masks[3:] + masks[2:3] + [1]
        for mask in order[1:-1]:
            other = swap(mine, mask, devices)
            mine = jnp.concatenate([mine, other], axis=0)
        other = swap(mine, order[-1], devices)
        base = call(
            functools.partial(base_kernel, order[:-1], width), [(spectral.shape, f32)], ins=[VMEM] * 3
        )(spectral, mine, other)[0]
    else:
        whole = lax.all_gather(momentum, AXES, axis=0, tiled=True)
        base = spectral - (learn_rate * decay_rate) * whole.T
    anchor = payload
    if devices & (devices - 1) == 0:
        for number, mask in enumerate(masks):
            payload = payload + swap(payload, mask, devices)
            if number == 0:
                anchor = payload
    else:
        payload = lax.psum(payload, AXES)
    field_now = call(field_kernel, [(velocity.shape, f32)], ins=[VMEM, VMEM, HBM])(previous, change, anchor)[0]
    groups = 4
    spectral_new, dense_new, momentum_new, trainer_loss = call(
        functools.partial(update_kernel, width, lines, groups),
        [(spectral.shape, f32), (dense.shape, f32), (momentum.shape, f32), ((1, 1), f32)],
        scratch=[
            pltpu.VMEM((LANES, LANES), f32), pltpu.VMEM(spectral.shape, f32), pltpu.VMEM(dense.shape, f32),
            pltpu.VMEM(momentum.shape, f32), pltpu.VMEM((1, 1), f32), pltpu.SemaphoreType.DMA((groups + 3,)),
        ],
        ins=[VMEM] * 6,
        places=[HBM] * 4,
    )(payload, spectral, base, dense, near_momentum, rows)
    return (field_now, trainer_loss, spectral_new.T, dense_new.T, momentum_new)


def solution(mesh):
    placed = (
        P("grp", "slab", None),
        P("grp", "slab", None),
        P("grp", "slab", None),
        P(("grp", "slab")),
        P(("grp", "slab")),
        P(("grp", "slab"), None),
        P(),
        P(),
        P(("grp", "slab"), None),
    )

    return jax.shard_map(
        local,
        mesh=mesh,
        in_specs=placed,
        out_specs=(P("grp", "slab", None), P("grp", "slab"), P(), P(), P(("grp", "slab"), None)),
        check_vma=False,
    )
```

```python
import functools
import math

import jax
import jax.numpy as jnp
import numpy as np
from jax import lax
from jax.experimental import pallas as pl
from jax.experimental.pallas import tpu as pltpu
from jax.sharding import PartitionSpec as P


SUB = 128
MODES = 16
LANES = 128
FEATURES = 2 * MODES + 8

decay_rate = 0.9
learn_rate = 0.5
dense_rate = 3.0

AXES = ("grp", "slab")
NT = (((1,), (1,)), ((), ()))
VMEM = pl.BlockSpec(memory_space=pltpu.VMEM)
HBM = pl.BlockSpec(memory_space=pltpu.HBM)


def call(kernel, outs, scratch=(), ins=(), places=None, flops=1000000):
    outs = [jax.ShapeDtypeStruct(shape, dtype) for shape, dtype in outs]
    size = sum(math.prod(o.shape) * o.dtype.itemsize for o in outs)
    return pl.pallas_call(
        kernel,
        out_shape=outs,
        in_specs=list(ins),
        out_specs=places or [VMEM] * len(outs),
        scratch_shapes=list(scratch),
        compiler_params=pltpu.CompilerParams(vmem_limit_bytes=16 << 20),
        cost_estimate=pl.CostEstimate(flops=flops, bytes_accessed=2 * size, transcendentals=0),
    )


def halves(array):
    coarse = array.astype(jnp.bfloat16).astype(jnp.float32)
    return coarse, array - coarse


def tables():
    counts = np.arange(SUB)
    waves = np.arange(MODES)
    angle = (waves[:, None] * counts[None, :] % SUB) * (2.0 * np.pi / SUB)
    weight = np.where(waves == 0, 1.0, 2.0)[:, None] / SUB
    plain = np.concatenate([np.cos(angle), np.sin(angle)]).astype(np.float32)
    parts = []
    rest = plain
    for _ in range(3):
        parts.append(rest.astype(jnp.bfloat16))
        rest = rest - parts[-1].astype(np.float32)
    high, middle, low = parts
    weighted = np.concatenate([weight * np.cos(angle), weight * np.sin(angle)]).astype(np.float32)
    return weighted, np.concatenate([high, high, middle, middle, high, low], axis=1)


def put_plane(ref, row, plane):
    for q in range(plane.shape[1] // LANES):
        ref[row + 8 * q : row + 8 * q + 8, :] = plane[:, q * LANES : (q + 1) * LANES]


def get_plane(ref, row, chunks):
    return jnp.concatenate([ref[row + 8 * q : row + 8 * q + 8, :] for q in range(chunks)], axis=1)


def pack_rows(block):
    half = block.shape[0] // 2
    return jnp.concatenate([block[:half], block[half:]], axis=1)


LAYERS = 3


def beside_in_z(plane):
    size = plane.shape[1]
    return pltpu.roll(plane, 1, 1) + pltpu.roll(plane, size - 1, 1)


def shifted(plane, before, after):
    sublane = lax.broadcasted_iota(jnp.int32, plane.shape, 0)
    last = plane.shape[0] - 1
    up = jnp.where(sublane == last, after, pltpu.roll(plane, last, 0))
    down = jnp.where(sublane == 0, before, pltpu.roll(plane, 1, 0))
    return up, down


def edge_kernel(with_momentum, sides, v_hbm, rate_hbm, forcing_hbm, momentum_hbm, *rest):
    v_ref, rate_ref, forcing_ref, momentum_ref, a_ref, b_ref = rest[:6]
    across = rest[6 : 6 + sides]
    corners_a = rest[6 + sides : 6 + 2 * sides]
    corners_b = rest[6 + 2 * sides : 6 + 3 * sides]
    sems = rest[-1]
    pairs = ((momentum_hbm, momentum_ref), (v_hbm, v_ref), (rate_hbm, rate_ref), (forcing_hbm, forcing_ref))
    moves = [pltpu.make_async_copy(*pair, sems.at[number]) for number, pair in enumerate(pairs)]
    for move in moves:
        move.start()
    last = v_ref.shape[0] - 1
    chunks = v_ref.shape[2] // LANES
    even = lax.rem(lax.axis_index("slab"), 2) == 0
    moves[0].wait()
    if with_momentum:
        packed = pack_rows(momentum_ref[...].T)
        start = LAYERS * 8 * chunks
        across[0][start : start + packed.shape[0], :] = packed
    for move in moves[1:]:
        move.wait()

    def message(edge, inside, rate, forcing):
        up, down = shifted(edge, 0.0, 0.0)
        partial = edge + (rate * (inside + up + down + beside_in_z(edge) - 6.0 * edge) + forcing)
        return edge, rate, partial

    highs = [lax.axis_index("grp") == 0] if sides == 1 else [True, False]
    for number, high in enumerate(highs):
        edge, inside = jnp.where(high, last, 0), jnp.where(high, last - 1, 1)
        planes = message(v_ref[edge], v_ref[inside], rate_ref[edge], forcing_ref[edge])
        for layer, plane in enumerate(planes):
            put_plane(across[number], layer * 8 * chunks, plane)
        left, right = planes[0][0:1], planes[0][planes[0].shape[0] - 1 :]
        for ref, line in (
            (corners_a[number], jnp.where(even, right, left)),
            (corners_b[number], jnp.where(even, left, right)),
        ):
            ref[...] = jnp.zeros_like(ref)
            for q in range(chunks):
                ref[q : q + 1, :] = line[:, q * LANES : (q + 1) * LANES]
    last = v_ref.shape[1] - 1
    lefts, rights = (
        message(v_ref[:, at, :], v_ref[:, inside, :], rate_ref[:, at, :], forcing_ref[:, at, :])
        for at, inside in ((0, 1), (last, last - 1))
    )
    for layer, (left, right) in enumerate(zip(lefts, rights)):
        put_plane(a_ref, layer * 8 * chunks, jnp.where(even, right, left))
        put_plane(b_ref, layer * 8 * chunks, jnp.where(even, left, right))


def grp_halo(two_sided, refs, layer, chunks):
    rows = 8 * chunks * layer
    if two_sided:
        return get_plane(refs[0], rows, chunks), get_plane(refs[1], rows, chunks)
    plane = get_plane(refs[0], rows, chunks)
    first = lax.axis_index("grp") == 0
    return jnp.where(first, 0.0, plane), jnp.where(first, plane, 0.0)


def as_row(column):
    size = column.shape[0]
    square = (size, size)
    same = lax.broadcasted_iota(jnp.int32, square, 0) == lax.broadcasted_iota(jnp.int32, square, 1)
    return jnp.sum(jnp.where(same, column, 0.0), axis=0, keepdims=True)


def feature_kernel(width, spectral_ref, dense_ref, map_ref, projection_ref, row_ref):
    gain = as_row(dense_ref[:, width : width + 1])
    bias = as_row(dense_ref[:, width + 1 : width + 2])
    projection_ref[...] = jnp.broadcast_to(dense_ref[:, width + 3 : width + 4], (width, LANES))
    row_ref[...] = jnp.zeros_like(row_ref)
    row_ref[0:1, :] = jnp.concatenate([gain, gain], axis=1)
    row_ref[1:2, :] = jnp.concatenate([bias, bias], axis=1)
    gains = row_ref[0:1, :]
    lane = lax.broadcasted_iota(jnp.int32, (width, LANES), 1)
    low = lane < width
    full = jnp.zeros((width, LANES), jnp.float32)
    for pair in range(MODES):
        product = spectral_ref[:, pair * LANES : (pair + 1) * LANES] * gains
        first = jnp.sum(jnp.where(low, product, 0.0), axis=1, keepdims=True)
        second = jnp.sum(jnp.where(low, 0.0, product), axis=1, keepdims=True)
        full = jnp.where(lane == 2 * pair, first, jnp.where(lane == 2 * pair + 1, second, full))
    mixing = dense_ref[:, 0:width]
    by_input = jnp.sum(gain * mixing, axis=1, keepdims=True)
    by_one = jnp.sum(bias * (mixing + spectral_ref[:, 0:width]), axis=1, keepdims=True)
    by_one = by_one + dense_ref[:, width + 2 : width + 3]
    full = jnp.where(lane == 2 * MODES, by_input, jnp.where(lane == 2 * MODES + 1, by_one, full))
    coarse = full.astype(jnp.bfloat16).astype(jnp.float32)
    fine = full - coarse
    joined = coarse + pltpu.roll(coarse, FEATURES, 1) + pltpu.roll(fine, 2 * FEATURES, 1)
    map_ref[...] = joined.astype(jnp.bfloat16)


def step_kernel(two_sided, width, scale, v_ref, rate_ref, forcing_ref, *refs):
    sides = 2 if two_sided else 1
    across, (a_ref, b_ref) = refs[:sides], refs[sides : sides + 2]
    corners_a, corners_b = refs[sides + 2 : 2 * sides + 2], refs[2 * sides + 2 : 3 * sides + 2]
    line_hbm, start_hbm, assign_hbm, map_ref, projection_ref, table_ref, wave_ref = refs[3 * sides + 2 : 3 * sides + 9]
    previous, change, pay_ref, line_ref, start_ref, assign_ref, sems = refs[3 * sides + 9 : 3 * sides + 16]
    inputs_ref, targets_ref, feature_ref, slope_ref = refs[3 * sides + 16 :]
    moves = [
        pltpu.make_async_copy(source, target, sems.at[number])
        for number, (source, target) in enumerate(
            ((line_hbm, line_ref), (start_hbm, start_ref), (assign_hbm, assign_ref))
        )
    ]
    for move in moves:
        move.start()
    cells_x, cells_y, cells_z = v_ref.shape
    chunks = cells_z // LANES
    slab = lax.axis_index("slab")
    even = lax.rem(slab, 2) == 0
    inner = jnp.logical_and(slab > 0, slab < lax.axis_size("slab") - 1)

    def slab_layer(layer):
        from_a = get_plane(a_ref, 8 * chunks * layer, chunks)
        from_b = jnp.where(inner, get_plane(b_ref, 8 * chunks * layer, chunks), 0.0)
        return jnp.where(even, from_b, from_a), jnp.where(even, from_a, from_b)

    def corner(side):
        here = True if two_sided else lax.axis_index("grp") == 1 - side

        def line(ref, valid):
            whole = jnp.concatenate([ref[q : q + 1, :] for q in range(chunks)], axis=1)
            return jnp.where(jnp.logical_and(here, valid), whole, 0.0)

        number = side if two_sided else 0
        from_a, from_b = line(corners_a[number], True), line(corners_b[number], inner)
        return jnp.where(even, from_b, from_a), jnp.where(even, from_a, from_b)

    def tendency(plane, above, below, up, down, rate, forcing):
        beside = above + below + up + down + beside_in_z(plane)
        return rate * (beside - 6.0 * plane) + forcing

    low, high = grp_halo(two_sided, across, 0, chunks)
    low_rate, high_rate = grp_halo(two_sided, across, 1, chunks)
    low_part, high_part = grp_halo(two_sided, across, 2, chunks)
    left, right = slab_layer(0)
    left_rate, right_rate = slab_layer(1)
    left_part, right_part = slab_layer(2)
    sublane = lax.broadcasted_iota(jnp.int32, (cells_y, cells_z), 0)

    def halo_step(part, rate, inner_plane, ends):
        last = part.shape[0] - 1
        at_ends = jnp.where(sublane == 0, ends[0], jnp.where(sublane == last, ends[1], 0.0))
        return part + rate * (inner_plane + at_ends)

    low_left, low_right = corner(0)
    high_left, high_right = corner(1)
    planes = [low] + [v_ref[i] for i in range(cells_x)] + [high]
    stepped = [halo_step(low_part, low_rate, planes[1], (low_left, low_right))]
    for i in range(cells_x):
        plane = planes[i + 1]
        up, down = shifted(plane, left[i : i + 1], right[i : i + 1])
        stepped.append(plane + tendency(plane, planes[i + 2], planes[i], up, down, rate_ref[i], forcing_ref[i]))
    stepped.append(halo_step(high_part, high_rate, planes[cells_x], (high_left, high_right)))
    left_new = halo_step(left_part, left_rate, v_ref[:, 0, :], (low_left, high_left))
    right_new = halo_step(right_part, right_rate, v_ref[:, cells_y - 1, :], (low_right, high_right))
    for i in range(cells_x):
        plane = stepped[i + 1]
        up, down = shifted(plane, left_new[i : i + 1], right_new[i : i + 1])
        moved = tendency(plane, stepped[i + 2], stepped[i], up, down, rate_ref[i], forcing_ref[i])
        previous[8 * i : 8 * i + 8, 0:cells_z] = plane
        change[8 * i : 8 * i + 8, 0:cells_z] = moved
    count = line_ref.shape[0]
    previous[:, cells_z : cells_z + LANES] = jnp.zeros((8 * cells_x, LANES), jnp.float32)
    change[:, cells_z : cells_z + LANES] = jnp.zeros((8 * cells_x, LANES), jnp.float32)
    for move in moves:
        move.wait()
    for t in range(count):
        line, start = line_ref[t], start_ref[t]
        inside = start & (LANES - 1)
        base = pl.multiple_of(start - inside, LANES)
        turn = (2 * LANES - inside) & (2 * LANES - 1)
        row = previous[pl.ds(line, 1), pl.ds(base, 2 * LANES)]
        inputs_ref[t : t + 1, :] = pltpu.roll(row, turn, 1)[:, :SUB]
        row = change[pl.ds(line, 1), pl.ds(base, 2 * LANES)]
        targets_ref[t : t + 1, :] = pltpu.roll(row, turn, 1)[:, :SUB]

    cos_w, sin_w = table_ref[0:MODES, :], table_ref[MODES:, :]
    coarse, rest = halves(inputs_ref[...])
    middle, fine = halves(rest)
    parts = jnp.concatenate([coarse, middle, coarse, middle, fine, coarse], axis=1).astype(jnp.bfloat16)
    waves = lax.dot_general(wave_ref[...], parts, NT, preferred_element_type=jnp.float32)
    tail = lax.broadcasted_iota(jnp.int32, (8, SUB), 0)
    half_projection = 0.5 * projection_ref[...]
    channel_map = map_ref[...]
    held = jnp.zeros((width, SUB), jnp.float32)
    lane = lax.broadcasted_iota(jnp.int32, (1, LANES), 1)
    losses = jnp.zeros((1, LANES), jnp.float32)
    root = math.sqrt(2.0 / math.pi)
    bend = 0.044715
    group = 4
    pairs = None
    for t in range(count):
        real, imag = waves[:MODES, t : t + 1], waves[MODES:, t : t + 1]
        line = inputs_ref[t : t + 1, :]
        rest = jnp.where(tail == 0, line, jnp.where(tail == 1, 1.0, 0.0))
        feature = jnp.concatenate([real * cos_w + imag * sin_w, imag * cos_w - real * sin_w, rest], axis=0)
        coarse, fine = halves(feature)
        zeros = jnp.zeros((LANES - 3 * FEATURES, SUB), jnp.float32)
        stack = jnp.concatenate([coarse, fine, coarse, zeros], axis=0).astype(jnp.bfloat16)
        at = slice(t % group * SUB, (t % group + 1) * SUB)
        feature_ref[t // group % 2, :, at] = stack
        before = jnp.dot(channel_map, stack, preferred_element_type=jnp.float32)
        square = before * before
        grown = 1.0 + jnp.tanh(before * (root + (root * bend) * square))
        after = before * grown
        slope = grown * (1.0 + (2.0 - grown) * (before * (root + (3.0 * root * bend) * square)))
        output = jnp.sum(after * half_projection, axis=0, keepdims=True)
        differ = output - targets_ref[t : t + 1, :]
        error = jnp.sum(differ * differ, axis=1, keepdims=True)
        losses = losses + jnp.where(lane == assign_ref[t], error, 0.0)
        pull = (2.0 * scale) * differ
        held = held + after * pull
        coarse, fine = halves(slope * (half_projection * pull))
        slope_ref[t // group % 2, 0:width, at] = coarse.astype(jnp.bfloat16)
        slope_ref[t // group % 2, width : 2 * width, at] = fine.astype(jnp.bfloat16)
        if (t + 1) % group == 0 or t + 1 == count:
            span = slice(0, (t % group + 1) * SUB)
            part = lax.dot_general(
                feature_ref[t // group % 2, :, span], slope_ref[t // group % 2, :, span], NT,
                preferred_element_type=jnp.float32,
            )[0 : 2 * FEATURES]
            pairs = part if pairs is None else pairs + part
    total = pairs[0:FEATURES, 0:width] + pairs[FEATURES : 2 * FEATURES, 0:width] + pairs[0:FEATURES, width:]
    pay_ref[...] = jnp.zeros_like(pay_ref)
    pay_ref[0:MODES, :] = jnp.concatenate([total[0:MODES], total[MODES : 2 * MODES]], axis=1)
    row = 2 * MODES
    pay_ref[MODES : MODES + 1, :] = jnp.concatenate([total[row : row + 1], total[row + 1 : row + 2]], axis=1)
    pay_ref[MODES + 1 : MODES + 2, 0:width] = as_row(0.5 * jnp.sum(held, axis=1, keepdims=True))
    pay_ref[pl.ds(MODES + 2 + lax.axis_index("grp"), 1), :] = losses


def field_kernel(previous, change, _, out_ref):
    cells_x, _, cells_z = out_ref.shape
    for i in range(cells_x):
        at = slice(8 * i, 8 * i + 8)
        out_ref[i] = previous[at, 0:cells_z] + change[at, 0:cells_z]


def base_kernel(masks, width, spectral_ref, mine_ref, other_ref, out_ref):
    here = lax.axis_index("grp") * lax.axis_size("slab") + lax.axis_index("slab")
    rows = width // 2
    low = lax.broadcasted_iota(jnp.int32, (rows, LANES), 1) < width
    for number in range(mine_ref.shape[0] // rows):
        source = here
        for bit, mask in enumerate(masks):
            if number >> bit & 1:
                source = source ^ mask
        even = lax.rem(source, 2) == 0
        columns = pl.ds(pl.multiple_of((source // 2) * LANES, LANES), LANES)
        mine = mine_ref[number * rows : (number + 1) * rows, :]
        other = other_ref[number * rows : (number + 1) * rows, :]
        first, second = jnp.where(even, mine, other), jnp.where(even, other, mine)
        top = jnp.where(low, first, pltpu.roll(second, width, 1))
        bottom = jnp.where(low, pltpu.roll(first, width, 1), second)
        factor = learn_rate * decay_rate
        out_ref[0:rows, columns] = spectral_ref[0:rows, columns] - factor * top
        out_ref[rows : 2 * rows, columns] = spectral_ref[rows : 2 * rows, columns] - factor * bottom


def prepare_kernel(width, spectral_ref, dense_ref, row_ref, spread_ref, turned_ref):
    tall = 2 * 8
    lane = lax.broadcasted_iota(jnp.int32, (tall, LANES), 1)
    row = lax.broadcasted_iota(jnp.int32, (tall, LANES), 0)
    low = lane < width
    gain, gain_rest = halves(learn_rate * row_ref[0:1, :])
    bias, bias_rest = halves(learn_rate * row_ref[1:2, :])
    parts = ((gain, bias), (gain_rest, bias_rest), (gain, bias))
    half = MODES // 2
    for pair in range(MODES):
        first = 2 * pair if pair < half else 2 * pair + 2
        for group in range(LANES // tall):
            block = jnp.zeros((tall, LANES), jnp.float32)
            for part, (gains, biases) in enumerate(parts):
                at = part * FEATURES + first - group * tall
                if -1 <= at < tall:
                    block = jnp.where(row == jnp.where(low, at, at + 1), gains, block)
                at = part * FEATURES + 2 * MODES + 2 - group * tall
                if pair == 0 and 0 <= at < tall:
                    block = jnp.where(jnp.logical_and(row == at, low), biases, block)
            columns = slice(pair * LANES, (pair + 1) * LANES)
            spread_ref[group * tall : (group + 1) * tall, columns] = block.astype(jnp.bfloat16)
    for pair in range(half):
        real = spectral_ref[:, pair * LANES : (pair + 1) * LANES].T
        imag = spectral_ref[:, (half + pair) * LANES : (half + pair + 1) * LANES].T
        turned_ref[pair * LANES : (pair + 1) * LANES, :] = jnp.concatenate([real, imag], axis=1)
    mixing = dense_ref[:, 0:width]
    both = jnp.concatenate([mixing, mixing + spectral_ref[:, 0:width]], axis=1).T
    turned_ref[MODES * width :, :] = jnp.concatenate([both[0:width], both[width:]], axis=1)


def update_kernel(
    width, lines, groups, pay_ref, base_ref, dense_ref, momentum_ref, row_ref, spread_ref, turned_ref,
    spectral_hbm, dense_hbm, momentum_hbm, loss_hbm, square, result, dense_out, momentum_out, loss_out, sems,
):
    first, second = lax.axis_index("grp"), lax.axis_index("slab")
    here = first * lax.axis_size("slab") + second
    copies = []

    def send(source, target):
        copies.append(pltpu.make_async_copy(source, target, sems.at[len(copies)]))
        copies[-1].start()

    kept = pay_ref.shape[0]
    square[0:kept, :] = pay_ref[...]
    square[kept:, :] = jnp.zeros((LANES - kept, LANES), jnp.float32)
    turned = square[...].T
    lane = lax.broadcasted_iota(jnp.int32, (width, LANES), 1)
    real, imag = turned[0:width], turned[width : 2 * width]
    factors = jnp.where(lane < MODES + 2, real, 0.0) + pltpu.roll(jnp.where(lane <= MODES, imag, 0.0), MODES + 2, 1)
    coarse, fine = halves(factors)
    stack = coarse + pltpu.roll(coarse, FEATURES, 1) + pltpu.roll(fine, 2 * FEATURES, 1)
    stack = stack.astype(jnp.bfloat16)
    columns = 2 * MODES * width // groups
    for group in range(groups):
        span = slice(group * columns, (group + 1) * columns)
        gradient = jnp.dot(stack, spread_ref[:, span], preferred_element_type=jnp.float32)
        result[:, span] = base_ref[:, span] - gradient
        send(result.at[:, pl.ds(group * columns, columns)], spectral_hbm.at[:, pl.ds(group * columns, columns)])

    slopes = pay_ref[MODES : MODES + 1, :]
    gain, bias = dense_ref[:, width : width + 1], dense_ref[:, width + 1 : width + 2]
    piece = momentum_ref.shape[0]
    block = here * piece // width
    inside = here * piece - block * width
    square[0:width, :] = jnp.where(lane < width, gain, bias)
    at = pl.ds(0 if piece == width else pl.multiple_of(inside, piece), piece)
    half = block // MODES
    row = pay_ref[pl.ds(block - half * MODES, 1), :]
    row = jnp.where(half == 0, row[:, 0:width], row[:, width:])
    gradient = square[at, 0:width] * row
    gradient = gradient + jnp.where(block == 0, square[at, width : 2 * width] * slopes[:, width:], 0.0)
    momentum_out[...] = decay_rate * momentum_ref[...] + gradient
    send(momentum_out, momentum_hbm)
    sums = pay_ref[pl.ds(MODES + 2 + first, 1), :]
    lane1 = lax.broadcasted_iota(jnp.int32, (1, LANES), 1)
    own = jnp.sum(jnp.where(lane1 == second, sums, 0.0), axis=1, keepdims=True)
    loss_out[...] = own * (1.0 / (lines * SUB))
    send(loss_out, loss_hbm)

    last = turned_ref[MODES * width :, :] * slopes
    gathered = jnp.where(lane < width, last, 0.0)
    for mode in range(MODES):
        gathered = gathered + turned_ref[mode * width : (mode + 1) * width, :] * pay_ref[mode : mode + 1, :]
    by_gain = jnp.sum(gathered, axis=1, keepdims=True)
    by_bias = jnp.sum(jnp.where(lane < width, 0.0, last), axis=1, keepdims=True)
    by_input, by_output, by_one = real[:, MODES : MODES + 1], real[:, MODES + 1 : MODES + 2], imag[:, MODES : MODES + 1]
    mixing = row_ref[0:1, 0:width] * by_input + row_ref[1:2, 0:width] * by_one
    dense_out[:, 0:width] = dense_ref[:, 0:width] - dense_rate * mixing
    lane4 = lax.broadcasted_iota(jnp.int32, (width, 4), 1)
    change = jnp.where(
        lane4 == 0, by_gain, jnp.where(lane4 == 1, by_bias, jnp.where(lane4 == 2, by_one, by_output)))
    dense_out[:, width : width + 4] = dense_ref[:, width : width + 4] - dense_rate * change
    send(dense_out, dense_hbm)
    for copy in copies:
        copy.wait()


def hop_masks(n_grp, n_slab):
    slab_bits = [1 << bit for bit in range(n_slab.bit_length() - 1)]
    grp_bits = [n_slab << bit for bit in range(n_grp.bit_length() - 1)]
    return [1] + [mask + 1 for mask in grp_bits + slab_bits[1:2] + slab_bits[:1:-1]]


def far_map(n_grp, n_slab):
    targets = {}
    for i in range(n_grp * n_slab):
        grp, slab = i // n_slab, i % n_slab
        if 0 < slab < n_slab - 1:
            targets[i] = i + 1 if slab % 2 else i - 1
        elif n_grp % 2 == 0:
            targets[i] = (grp ^ 1) * n_slab + slab
    return targets


def hop(array, targets):
    return lax.ppermute(array, AXES, sorted(targets.items()))


def in_hbm(array):
    return pltpu.with_memory_space_constraint(array, pltpu.HBM)


def swap(array, mask, count):
    return lax.ppermute(array, AXES, [(i, i ^ mask) for i in range(count)])


def local(velocity, rate, forcing, anchor_line, anchor_z, assign, spectral, dense, momentum):
    n_grp, n_slab = lax.axis_size("grp"), lax.axis_size("slab")
    devices = n_grp * n_slab
    width = dense.shape[1]
    lines = anchor_line.shape[0]
    cells_x, _, cells_z = velocity.shape
    chunks = cells_z // LANES
    halo_rows = LAYERS * 8 * chunks
    piece = momentum.shape[0]
    packed = piece // 2
    f32 = jnp.float32
    joined = n_grp == 2 and piece == width and devices & (devices - 1) == 0
    two_sided = n_grp != 2
    table, wave_table = (jnp.asarray(array) for array in tables())
    spectral, dense = spectral.T, dense.T

    sides = 2 if two_sided else 1
    edge_rows = halo_rows + (packed if joined else 0)
    message = ((halo_rows, LANES), f32)
    corner_message = ((-(-chunks // 8) * 8, LANES), f32)
    velocity, rate, forcing, near_momentum, to_a, to_b, *edges = call(
        functools.partial(edge_kernel, joined, sides),
        [(velocity.shape, f32)] * 3 + [(momentum.shape, f32), message, message]
        + [((edge_rows, LANES), f32)] * sides + [corner_message] * (2 * sides),
        scratch=[pltpu.SemaphoreType.DMA((4,))],
        ins=[HBM] * 4,
    )(*(in_hbm(array) for array in (velocity, rate, forcing, momentum)))
    far = far_map(n_grp, n_slab)
    near = {i: i ^ 1 for i in range(devices)}
    if two_sided:
        moves = [{i: i + n_slab for i in range(devices - n_slab)}, {i: i - n_slab for i in range(n_slab, devices)}]
        inner = [i for i in range(devices) if 0 < i % n_slab < n_slab - 1]
        diagonal_far = [{i: far[move[i]] for i in inner if i in move} for move in moves]
    else:
        moves = [{i: i ^ n_slab for i in range(devices)}]
        ends = (0, n_slab - 1)
        diagonal_far = [{i: i ^ n_slab if i % n_slab in ends else far[i ^ n_slab] for i in range(devices)}]
    from_grp = [hop(array, move) for array, move in zip(edges, moves)]
    from_b = hop(to_b, far)
    corners_b = [hop(array, move) for array, move in zip(edges[2 * sides :], diagonal_far)]
    corners_a = [
        hop(array, {i: j ^ 1 for i, j in move.items()}) for array, move in zip(edges[sides : 2 * sides], moves)
    ]
    from_a = hop(to_a, near)
    channel_map, projection, rows = call(
        functools.partial(feature_kernel, width),
        [((width, LANES), jnp.bfloat16), ((width, LANES), f32), ((8, LANES), f32)],
        ins=[VMEM] * 2,
    )(spectral, dense)
    pay_rows = -(-(MODES + 2 + n_grp) // 8) * 8
    scale = 1.0 / (devices * lines * SUB)
    window = ((8 * cells_x, cells_z + LANES), f32)
    previous, change, payload = call(
        functools.partial(step_kernel, two_sided, width, scale),
        [window, window, ((pay_rows, LANES), f32)],
        scratch=[pltpu.SMEM((lines,), jnp.int32)] * 3 + [
            pltpu.SemaphoreType.DMA((3,)),
            pltpu.VMEM((lines, SUB), f32),
            pltpu.VMEM((lines, SUB), f32),
            pltpu.VMEM((2, LANES, 4 * SUB), jnp.bfloat16),
            pltpu.VMEM((2, 2 * width, 4 * SUB), jnp.bfloat16),
        ],
        ins=[VMEM] * (5 + 3 * sides) + [HBM] * 3 + [VMEM] * 4,
    )(velocity, rate, forcing, *from_grp, from_a, from_b, *corners_a, *corners_b,
      in_hbm(anchor_line), in_hbm(anchor_z), in_hbm(assign.reshape(-1)), channel_map, projection, table, wave_table)

    masks = hop_masks(n_grp, n_slab)
    if joined:
        mine = jnp.concatenate([edges[0][halo_rows:], from_grp[0][halo_rows:]], axis=0)
        order = [n_slab] + masks[3:] + masks[2:3] + [1]
        for mask in order[1:-1]:
            other = swap(mine, mask, devices)
            mine = jnp.concatenate([mine, other], axis=0)
        other = swap(mine, order[-1], devices)
        base = call(
            functools.partial(base_kernel, order[:-1], width), [(spectral.shape, f32)], ins=[VMEM] * 3
        )(spectral, mine, other)[0]
    else:
        whole = lax.all_gather(momentum, AXES, axis=0, tiled=True)
        base = spectral - (learn_rate * decay_rate) * whole.T
    anchor = payload
    if devices & (devices - 1) == 0:
        for number, mask in enumerate(masks):
            payload = payload + swap(payload, mask, devices)
            if number == 0:
                anchor = payload
    else:
        payload = lax.psum(payload, AXES)
    field_now = call(field_kernel, [(velocity.shape, f32)], ins=[VMEM, VMEM, HBM])(previous, change, anchor)[0]
    spread, turned = call(
        functools.partial(prepare_kernel, width),
        [((LANES, 2 * MODES * width), jnp.bfloat16), (((MODES + 1) * width, LANES), f32)],
        ins=[VMEM] * 3,
    )(spectral, dense, rows)
    groups = 4
    spectral_new, dense_new, momentum_new, trainer_loss = call(
        functools.partial(update_kernel, width, lines, groups),
        [(spectral.shape, f32), (dense.shape, f32), (momentum.shape, f32), ((1, 1), f32)],
        scratch=[
            pltpu.VMEM((LANES, LANES), f32), pltpu.VMEM(spectral.shape, f32), pltpu.VMEM(dense.shape, f32),
            pltpu.VMEM(momentum.shape, f32), pltpu.VMEM((1, 1), f32), pltpu.SemaphoreType.DMA((groups + 3,)),
        ],
        ins=[VMEM] * 7,
        places=[HBM] * 4,
    )(payload, base, dense, near_momentum, rows, spread, turned)
    return (field_now, trainer_loss, spectral_new.T, dense_new.T, momentum_new)


def solution(mesh):
    placed = (
        P("grp", "slab", None),
        P("grp", "slab", None),
        P("grp", "slab", None),
        P(("grp", "slab")),
        P(("grp", "slab")),
        P(("grp", "slab"), None),
        P(),
        P(),
        P(("grp", "slab"), None),
    )

    return jax.shard_map(
        local,
        mesh=mesh,
        in_specs=placed,
        out_specs=(P("grp", "slab", None), P("grp", "slab"), P(), P(), P(("grp", "slab"), None)),
        check_vma=False,
    )
```

```python
import functools
import math

import jax
import jax.numpy as jnp
import numpy as np
from jax import lax
from jax.experimental import pallas as pl
from jax.experimental.pallas import tpu as pltpu
from jax.sharding import PartitionSpec as P


SUB = 128
MODES = 16
LANES = 128
FEATURES = 2 * MODES + 8

decay_rate = 0.9
learn_rate = 0.5
dense_rate = 3.0

AXES = ("grp", "slab")
NT = (((1,), (1,)), ((), ()))
VMEM = pl.BlockSpec(memory_space=pltpu.VMEM)
HBM = pl.BlockSpec(memory_space=pltpu.HBM)


def call(kernel, outs, scratch=(), ins=(), places=None, flops=1000000):
    outs = [jax.ShapeDtypeStruct(shape, dtype) for shape, dtype in outs]
    size = sum(math.prod(o.shape) * o.dtype.itemsize for o in outs)
    return pl.pallas_call(
        kernel,
        out_shape=outs,
        in_specs=list(ins),
        out_specs=places or [VMEM] * len(outs),
        scratch_shapes=list(scratch),
        compiler_params=pltpu.CompilerParams(vmem_limit_bytes=16 << 20),
        cost_estimate=pl.CostEstimate(flops=flops, bytes_accessed=2 * size, transcendentals=0),
    )


def halves(array):
    coarse = array.astype(jnp.bfloat16).astype(jnp.float32)
    return coarse, array - coarse


def tables():
    counts = np.arange(SUB)
    waves = np.arange(MODES)
    angle = (waves[:, None] * counts[None, :] % SUB) * (2.0 * np.pi / SUB)
    weight = np.where(waves == 0, 1.0, 2.0)[:, None] / SUB
    plain = np.concatenate([np.cos(angle), np.sin(angle)]).astype(np.float32)
    parts = []
    rest = plain
    for _ in range(3):
        parts.append(rest.astype(jnp.bfloat16))
        rest = rest - parts[-1].astype(np.float32)
    high, middle, low = parts
    weighted = np.concatenate([weight * np.cos(angle), weight * np.sin(angle)]).astype(np.float32)
    return weighted, np.concatenate([high, high, middle, middle, high, low], axis=1)


def put_plane(ref, row, plane):
    for q in range(plane.shape[1] // LANES):
        ref[row + 8 * q : row + 8 * q + 8, :] = plane[:, q * LANES : (q + 1) * LANES]


def get_plane(ref, row, chunks):
    return jnp.concatenate([ref[row + 8 * q : row + 8 * q + 8, :] for q in range(chunks)], axis=1)


def put_line(ref, row, line):
    for q in range(line.shape[1] // LANES):
        ref[row + q : row + q + 1, :] = line[:, q * LANES : (q + 1) * LANES]


def get_line(ref, row, chunks):
    return jnp.concatenate([ref[row + q : row + q + 1, :] for q in range(chunks)], axis=1)


def pack_rows(block):
    half = block.shape[0] // 2
    return jnp.concatenate([block[:half], block[half:]], axis=1)


LAYERS = 3


def beside_in_z(plane):
    size = plane.shape[1]
    return pltpu.roll(plane, 1, 1) + pltpu.roll(plane, size - 1, 1)


def shifted(plane, before, after):
    sublane = lax.broadcasted_iota(jnp.int32, plane.shape, 0)
    last = plane.shape[0] - 1
    up = jnp.where(sublane == last, after, pltpu.roll(plane, last, 0))
    down = jnp.where(sublane == 0, before, pltpu.roll(plane, 1, 0))
    return up, down


def edge_kernel(
    with_momentum, sides, v_hbm, rate_hbm, forcing_hbm, momentum_hbm, dense_hbm, table_hbm, wave_hbm, *rest
):
    v_ref, rate_ref, forcing_ref, momentum_ref, dense_ref, table_ref, wave_ref, a_ref, b_ref = rest[:9]
    rest = rest[3:]
    across = rest[6 : 6 + sides]
    corners = rest[6 + sides : 6 + 2 * sides]
    sems = rest[-1]
    pairs = (
        (momentum_hbm, momentum_ref), (v_hbm, v_ref), (rate_hbm, rate_ref), (forcing_hbm, forcing_ref),
        (dense_hbm, dense_ref), (table_hbm, table_ref), (wave_hbm, wave_ref),
    )
    moves = [pltpu.make_async_copy(*pair, sems.at[number]) for number, pair in enumerate(pairs)]
    for move in moves:
        move.start()
    last = v_ref.shape[0] - 1
    chunks = v_ref.shape[2] // LANES
    even = lax.rem(lax.axis_index("slab"), 2) == 0
    moves[0].wait()
    if with_momentum:
        packed = pack_rows(momentum_ref[...].T)
        start = LAYERS * 8 * chunks
        across[0][start : start + packed.shape[0], :] = packed
    for move in moves[1:]:
        move.wait()

    def message(edge, inside, rate, forcing):
        up, down = shifted(edge, 0.0, 0.0)
        partial = edge + (rate * (inside + up + down + beside_in_z(edge) - 6.0 * edge) + forcing)
        return edge, rate, partial

    highs = [lax.axis_index("grp") == 0] if sides == 1 else [True, False]
    for number, high in enumerate(highs):
        edge, inside = jnp.where(high, last, 0), jnp.where(high, last - 1, 1)
        planes = message(v_ref[edge], v_ref[inside], rate_ref[edge], forcing_ref[edge])
        for layer, plane in enumerate(planes):
            put_plane(across[number], layer * 8 * chunks, plane)
        left, right = planes[0][0:1], planes[0][planes[0].shape[0] - 1 :]
        corners[number][...] = jnp.zeros_like(corners[number])
        put_line(corners[number], 0, jnp.where(even, left, right))
    last = v_ref.shape[1] - 1
    lefts, rights = (
        message(v_ref[:, at, :], v_ref[:, inside, :], rate_ref[:, at, :], forcing_ref[:, at, :])
        for at, inside in ((0, 1), (last, last - 1))
    )
    for layer, (left, right) in enumerate(zip(lefts, rights)):
        put_plane(a_ref, layer * 8 * chunks, jnp.where(even, right, left))
        put_plane(b_ref, layer * 8 * chunks, jnp.where(even, left, right))


def grp_halo(two_sided, refs, layer, chunks):
    rows = 8 * chunks * layer
    if two_sided:
        return get_plane(refs[0], rows, chunks), get_plane(refs[1], rows, chunks)
    plane = get_plane(refs[0], rows, chunks)
    first = lax.axis_index("grp") == 0
    return jnp.where(first, 0.0, plane), jnp.where(first, plane, 0.0)


def near_kernel(sides, chunks, message_ref, *refs):
    across, out_ref = refs[:sides], refs[sides]
    even = lax.rem(lax.axis_index("slab"), 2) == 0
    rows = message_ref.shape[0]
    out_ref[0:rows, :] = message_ref[...]
    out_ref[rows:, :] = jnp.zeros((out_ref.shape[0] - rows, LANES), jnp.float32)
    for number in range(sides):
        plane = get_plane(across[number], 0, chunks)
        last = plane.shape[0] - 1
        put_line(out_ref, rows + number * chunks, jnp.where(even, plane[last:], plane[0:1]))


def as_row(column):
    size = column.shape[0]
    square = (size, size)
    same = lax.broadcasted_iota(jnp.int32, square, 0) == lax.broadcasted_iota(jnp.int32, square, 1)
    return jnp.sum(jnp.where(same, column, 0.0), axis=0, keepdims=True)


def feature_map(width, spectral_ref, dense_ref):
    gain = as_row(dense_ref[:, width : width + 1])
    bias = as_row(dense_ref[:, width + 1 : width + 2])
    gains = jnp.concatenate([gain, gain], axis=1)
    lane = lax.broadcasted_iota(jnp.int32, (width, LANES), 1)
    low = lane < width
    full = jnp.zeros((width, LANES), jnp.float32)
    for pair in range(MODES):
        product = spectral_ref[:, pair * LANES : (pair + 1) * LANES] * gains
        first = jnp.sum(jnp.where(low, product, 0.0), axis=1, keepdims=True)
        second = jnp.sum(jnp.where(low, 0.0, product), axis=1, keepdims=True)
        full = jnp.where(lane == 2 * pair, first, jnp.where(lane == 2 * pair + 1, second, full))
    mixing = dense_ref[:, 0:width]
    by_input = jnp.sum(gain * mixing, axis=1, keepdims=True)
    by_one = jnp.sum(bias * (mixing + spectral_ref[:, 0:width]), axis=1, keepdims=True)
    by_one = by_one + dense_ref[:, width + 2 : width + 3]
    full = jnp.where(lane == 2 * MODES, by_input, jnp.where(lane == 2 * MODES + 1, by_one, full))
    coarse, fine = halves(full)
    joined = coarse + pltpu.roll(coarse, FEATURES, 1) + pltpu.roll(fine, 2 * FEATURES, 1)
    return joined.astype(jnp.bfloat16)


def step_kernel(two_sided, width, scale, v_ref, rate_ref, forcing_ref, *refs):
    sides = 2 if two_sided else 1
    across, (a_ref, b_ref) = refs[:sides], refs[sides : sides + 2]
    corners, refs = refs[sides + 2 : 2 * sides + 2], refs[2 * sides + 2 :]
    line_hbm, start_hbm, assign_hbm, spectral_ref, dense_ref, table_ref, wave_ref = refs[:7]
    previous, change, pay_ref, line_ref, start_ref, assign_ref, sems = refs[7:14]
    inputs_ref, feature_ref, slope_ref = refs[14:]
    moves = [
        pltpu.make_async_copy(source, target, sems.at[number])
        for number, (source, target) in enumerate(
            ((line_hbm, line_ref), (start_hbm, start_ref), (assign_hbm, assign_ref))
        )
    ]
    for move in moves:
        move.start()
    cells_x, cells_y, cells_z = v_ref.shape
    chunks = cells_z // LANES
    slab = lax.axis_index("slab")
    even = lax.rem(slab, 2) == 0
    inner = jnp.logical_and(slab > 0, slab < lax.axis_size("slab") - 1)

    def slab_layer(layer):
        from_a = get_plane(a_ref, 8 * chunks * layer, chunks)
        from_b = jnp.where(inner, get_plane(b_ref, 8 * chunks * layer, chunks), 0.0)
        return jnp.where(even, from_b, from_a), jnp.where(even, from_a, from_b)

    def corner(side):
        here = True if two_sided else lax.axis_index("grp") == 1 - side

        number = side if two_sided else 0
        from_a = get_line(a_ref, LAYERS * 8 * chunks + number * chunks, chunks)
        from_b = get_line(corners[number], 0, chunks)
        from_a = jnp.where(here, from_a, 0.0)
        from_b = jnp.where(jnp.logical_and(here, inner), from_b, 0.0)
        return jnp.where(even, from_b, from_a), jnp.where(even, from_a, from_b)

    def tendency(plane, above, below, up, down, rate, forcing):
        beside = above + below + up + down + beside_in_z(plane)
        return rate * (beside - 6.0 * plane) + forcing

    low, high = grp_halo(two_sided, across, 0, chunks)
    low_rate, high_rate = grp_halo(two_sided, across, 1, chunks)
    low_part, high_part = grp_halo(two_sided, across, 2, chunks)
    left, right = slab_layer(0)
    left_rate, right_rate = slab_layer(1)
    left_part, right_part = slab_layer(2)
    sublane = lax.broadcasted_iota(jnp.int32, (cells_y, cells_z), 0)

    def halo_step(part, rate, inner_plane, ends):
        last = part.shape[0] - 1
        at_ends = jnp.where(sublane == 0, ends[0], jnp.where(sublane == last, ends[1], 0.0))
        return part + rate * (inner_plane + at_ends)

    low_left, low_right = corner(0)
    high_left, high_right = corner(1)
    planes = [low] + [v_ref[i] for i in range(cells_x)] + [high]
    stepped = [halo_step(low_part, low_rate, planes[1], (low_left, low_right))]
    for i in range(cells_x):
        plane = planes[i + 1]
        up, down = shifted(plane, left[i : i + 1], right[i : i + 1])
        stepped.append(plane + tendency(plane, planes[i + 2], planes[i], up, down, rate_ref[i], forcing_ref[i]))
    stepped.append(halo_step(high_part, high_rate, planes[cells_x], (high_left, high_right)))
    left_new = halo_step(left_part, left_rate, v_ref[:, 0, :], (low_left, high_left))
    right_new = halo_step(right_part, right_rate, v_ref[:, cells_y - 1, :], (low_right, high_right))
    for i in range(cells_x):
        plane = stepped[i + 1]
        up, down = shifted(plane, left_new[i : i + 1], right_new[i : i + 1])
        moved = tendency(plane, stepped[i + 2], stepped[i], up, down, rate_ref[i], forcing_ref[i])
        previous[8 * i : 8 * i + 8, 0:cells_z] = plane
        change[8 * i : 8 * i + 8, 0:cells_z] = moved
    count = line_ref.shape[0]
    previous[:, cells_z : cells_z + LANES] = jnp.zeros((8 * cells_x, LANES), jnp.float32)
    change[:, cells_z : cells_z + LANES] = jnp.zeros((8 * cells_x, LANES), jnp.float32)
    channel_map = feature_map(width, spectral_ref, dense_ref)
    for move in moves:
        move.wait()

    def window(ref, t):
        line, start = line_ref[t], start_ref[t]
        inside = start & (LANES - 1)
        base = pl.multiple_of(start - inside, LANES)
        row = ref[pl.ds(line, 1), pl.ds(base, 2 * LANES)]
        return pltpu.roll(row, (2 * LANES - inside) & (2 * LANES - 1), 1)[:, :SUB]

    for t in range(count):
        inputs_ref[t : t + 1, :] = window(previous, t)

    cos_w, sin_w = table_ref[0:MODES, :], table_ref[MODES:, :]
    coarse, rest = halves(inputs_ref[...])
    middle, fine = halves(rest)
    parts = jnp.concatenate([coarse, middle, coarse, middle, fine, coarse], axis=1).astype(jnp.bfloat16)
    waves = lax.dot_general(wave_ref[...], parts, NT, preferred_element_type=jnp.float32)
    tail = lax.broadcasted_iota(jnp.int32, (8, SUB), 0)
    half_projection = jnp.broadcast_to(0.5 * dense_ref[:, width + 3 : width + 4], (width, SUB))
    held = jnp.zeros((width, SUB), jnp.float32)
    lane = lax.broadcasted_iota(jnp.int32, (1, LANES), 1)
    losses = jnp.zeros((1, LANES), jnp.float32)
    root = math.sqrt(2.0 / math.pi)
    bend = 0.044715
    group = 2
    pairs = None
    for t in range(count):
        real, imag = waves[:MODES, t : t + 1], waves[MODES:, t : t + 1]
        line = inputs_ref[t : t + 1, :]
        rest = jnp.where(tail == 0, line, jnp.where(tail == 1, 1.0, 0.0))
        feature = jnp.concatenate([real * cos_w + imag * sin_w, imag * cos_w - real * sin_w, rest], axis=0)
        coarse, fine = halves(feature)
        zeros = jnp.zeros((LANES - 3 * FEATURES, SUB), jnp.float32)
        stack = jnp.concatenate([coarse, fine, coarse, zeros], axis=0).astype(jnp.bfloat16)
        at = slice(t % group * SUB, (t % group + 1) * SUB)
        feature_ref[t // group % 2, :, at] = stack
        before = jnp.dot(channel_map, stack, preferred_element_type=jnp.float32)
        square = before * before
        grown = 1.0 + jnp.tanh(before * (root + (root * bend) * square))
        after = before * grown
        slope = grown * (1.0 + (2.0 - grown) * (before * (root + (3.0 * root * bend) * square)))
        output = jnp.sum(after * half_projection, axis=0, keepdims=True)
        differ = output - window(change, t)
        error = jnp.sum(differ * differ, axis=1, keepdims=True)
        losses = losses + jnp.where(lane == assign_ref[t], error, 0.0)
        pull = (2.0 * scale) * differ
        held = held + after * pull
        coarse, fine = halves(slope * (half_projection * pull))
        slope_ref[t // group % 2, 0:width, at] = coarse.astype(jnp.bfloat16)
        slope_ref[t // group % 2, width : 2 * width, at] = fine.astype(jnp.bfloat16)
        if (t + 1) % group == 0 or t + 1 == count:
            span = slice(0, (t % group + 1) * SUB)
            part = lax.dot_general(
                feature_ref[t // group % 2, :, span], slope_ref[t // group % 2, :, span], NT,
                preferred_element_type=jnp.float32,
            )[0 : 2 * FEATURES]
            pairs = part if pairs is None else pairs + part
    total = pairs[0:FEATURES, 0:width] + pairs[FEATURES : 2 * FEATURES, 0:width] + pairs[0:FEATURES, width:]
    pay_ref[...] = jnp.zeros_like(pay_ref)
    pay_ref[0:MODES, :] = jnp.concatenate([total[0:MODES], total[MODES : 2 * MODES]], axis=1)
    row = 2 * MODES
    pay_ref[MODES : MODES + 1, :] = jnp.concatenate([total[row : row + 1], total[row + 1 : row + 2]], axis=1)
    pay_ref[MODES + 1 : MODES + 2, 0:width] = as_row(0.5 * jnp.sum(held, axis=1, keepdims=True))
    pay_ref[pl.ds(MODES + 2 + lax.axis_index("grp"), 1), :] = losses


def field_kernel(previous, change, _, out_ref):
    cells_x, _, cells_z = out_ref.shape
    for i in range(cells_x):
        at = slice(8 * i, 8 * i + 8)
        out_ref[i] = previous[at, 0:cells_z] + change[at, 0:cells_z]


def base_kernel(masks, width, spectral_ref, mine_ref, other_ref, out_ref):
    here = lax.axis_index("grp") * lax.axis_size("slab") + lax.axis_index("slab")
    rows = width // 2
    low = lax.broadcasted_iota(jnp.int32, (rows, LANES), 1) < width
    for number in range(mine_ref.shape[0] // rows):
        source = here
        for bit, mask in enumerate(masks):
            if number >> bit & 1:
                source = source ^ mask
        even = lax.rem(source, 2) == 0
        columns = pl.ds(pl.multiple_of((source // 2) * LANES, LANES), LANES)
        mine = mine_ref[number * rows : (number + 1) * rows, :]
        other = other_ref[number * rows : (number + 1) * rows, :]
        first, second = jnp.where(even, mine, other), jnp.where(even, other, mine)
        top = jnp.where(low, first, pltpu.roll(second, width, 1))
        bottom = jnp.where(low, pltpu.roll(first, width, 1), second)
        factor = learn_rate * decay_rate
        out_ref[0:rows, columns] = spectral_ref[0:rows, columns] - factor * top
        out_ref[rows : 2 * rows, columns] = spectral_ref[rows : 2 * rows, columns] - factor * bottom


def prepare_kernel(width, spectral_ref, dense_ref, row_ref, spread_ref, turned_ref):
    row_ref[...] = jnp.zeros_like(row_ref)
    for number in range(2):
        row = as_row(dense_ref[:, width + number : width + number + 1])
        row_ref[number : number + 1, :] = jnp.concatenate([row, row], axis=1)
    tall = 2 * 8
    lane = lax.broadcasted_iota(jnp.int32, (tall, LANES), 1)
    row = lax.broadcasted_iota(jnp.int32, (tall, LANES), 0)
    low = lane < width
    gain, gain_rest = halves(learn_rate * row_ref[0:1, :])
    bias, bias_rest = halves(learn_rate * row_ref[1:2, :])
    parts = ((gain, bias), (gain_rest, bias_rest), (gain, bias))
    half = MODES // 2
    for pair in range(MODES):
        first = 2 * pair if pair < half else 2 * pair + 2
        for group in range(LANES // tall):
            block = jnp.zeros((tall, LANES), jnp.float32)
            for part, (gains, biases) in enumerate(parts):
                at = part * FEATURES + first - group * tall
                if -1 <= at < tall:
                    block = jnp.where(row == jnp.where(low, at, at + 1), gains, block)
                at = part * FEATURES + 2 * MODES + 2 - group * tall
                if pair == 0 and 0 <= at < tall:
                    block = jnp.where(jnp.logical_and(row == at, low), biases, block)
            columns = slice(pair * LANES, (pair + 1) * LANES)
            spread_ref[group * tall : (group + 1) * tall, columns] = block.astype(jnp.bfloat16)
    for pair in range(half):
        real = spectral_ref[:, pair * LANES : (pair + 1) * LANES].T
        imag = spectral_ref[:, (half + pair) * LANES : (half + pair + 1) * LANES].T
        turned_ref[pair * LANES : (pair + 1) * LANES, :] = jnp.concatenate([real, imag], axis=1)
    mixing = dense_ref[:, 0:width]
    both = jnp.concatenate([mixing, mixing + spectral_ref[:, 0:width]], axis=1).T
    turned_ref[MODES * width :, :] = jnp.concatenate([both[0:width], both[width:]], axis=1)


def update_kernel(
    width, lines, groups, pay_ref, base_ref, dense_ref, momentum_ref, row_ref, spread_ref, turned_ref,
    spectral_hbm, dense_hbm, momentum_hbm, loss_hbm, square, result, dense_out, momentum_out, loss_out, sems,
):
    first, second = lax.axis_index("grp"), lax.axis_index("slab")
    here = first * lax.axis_size("slab") + second
    copies = []

    def send(source, target):
        copies.append(pltpu.make_async_copy(source, target, sems.at[len(copies)]))
        copies[-1].start()

    kept = pay_ref.shape[0]
    square[0:kept, :] = pay_ref[...]
    square[kept:, :] = jnp.zeros((LANES - kept, LANES), jnp.float32)
    turned = square[...].T
    lane = lax.broadcasted_iota(jnp.int32, (width, LANES), 1)
    real, imag = turned[0:width], turned[width : 2 * width]
    factors = jnp.where(lane < MODES + 2, real, 0.0) + pltpu.roll(jnp.where(lane <= MODES, imag, 0.0), MODES + 2, 1)
    coarse, fine = halves(factors)
    stack = coarse + pltpu.roll(coarse, FEATURES, 1) + pltpu.roll(fine, 2 * FEATURES, 1)
    stack = stack.astype(jnp.bfloat16)
    columns = 2 * MODES * width // groups
    for group in range(groups):
        span = slice(group * columns, (group + 1) * columns)
        gradient = jnp.dot(stack, spread_ref[:, span], preferred_element_type=jnp.float32)
        result[:, span] = base_ref[:, span] - gradient
        send(result.at[:, pl.ds(group * columns, columns)], spectral_hbm.at[:, pl.ds(group * columns, columns)])

    slopes = pay_ref[MODES : MODES + 1, :]
    gain, bias = dense_ref[:, width : width + 1], dense_ref[:, width + 1 : width + 2]
    piece = momentum_ref.shape[0]
    block = here * piece // width
    inside = here * piece - block * width
    square[0:width, :] = jnp.where(lane < width, gain, bias)
    at = pl.ds(0 if piece == width else pl.multiple_of(inside, piece), piece)
    half = block // MODES
    row = pay_ref[pl.ds(block - half * MODES, 1), :]
    row = jnp.where(half == 0, row[:, 0:width], row[:, width:])
    gradient = square[at, 0:width] * row
    gradient = gradient + jnp.where(block == 0, square[at, width : 2 * width] * slopes[:, width:], 0.0)
    momentum_out[...] = decay_rate * momentum_ref[...] + gradient
    send(momentum_out, momentum_hbm)
    sums = pay_ref[pl.ds(MODES + 2 + first, 1), :]
    lane1 = lax.broadcasted_iota(jnp.int32, (1, LANES), 1)
    own = jnp.sum(jnp.where(lane1 == second, sums, 0.0), axis=1, keepdims=True)
    loss_out[...] = own * (1.0 / (lines * SUB))
    send(loss_out, loss_hbm)

    last = turned_ref[MODES * width :, :] * slopes
    gathered = jnp.where(lane < width, last, 0.0)
    for mode in range(MODES):
        gathered = gathered + turned_ref[mode * width : (mode + 1) * width, :] * pay_ref[mode : mode + 1, :]
    by_gain = jnp.sum(gathered, axis=1, keepdims=True)
    by_bias = jnp.sum(jnp.where(lane < width, 0.0, last), axis=1, keepdims=True)
    by_input, by_output, by_one = real[:, MODES : MODES + 1], real[:, MODES + 1 : MODES + 2], imag[:, MODES : MODES + 1]
    mixing = row_ref[0:1, 0:width] * by_input + row_ref[1:2, 0:width] * by_one
    dense_out[:, 0:width] = dense_ref[:, 0:width] - dense_rate * mixing
    lane4 = lax.broadcasted_iota(jnp.int32, (width, 4), 1)
    change = jnp.where(
        lane4 == 0, by_gain, jnp.where(lane4 == 1, by_bias, jnp.where(lane4 == 2, by_one, by_output)))
    dense_out[:, width : width + 4] = dense_ref[:, width : width + 4] - dense_rate * change
    send(dense_out, dense_hbm)
    for copy in copies:
        copy.wait()


def hop_masks(n_grp, n_slab):
    slab_bits = [1 << bit for bit in range(n_slab.bit_length() - 1)]
    grp_bits = [n_slab << bit for bit in range(n_grp.bit_length() - 1)]
    return [1] + [mask + 1 for mask in grp_bits + slab_bits[1:2] + slab_bits[:1:-1]]


def far_map(n_grp, n_slab):
    targets = {}
    for i in range(n_grp * n_slab):
        grp, slab = i // n_slab, i % n_slab
        if 0 < slab < n_slab - 1:
            targets[i] = i + 1 if slab % 2 else i - 1
        elif n_grp % 2 == 0:
            targets[i] = (grp ^ 1) * n_slab + slab
    return targets


def hop(array, targets):
    return lax.ppermute(array, AXES, sorted(targets.items()))


def in_hbm(array):
    return pltpu.with_memory_space_constraint(array, pltpu.HBM)


def swap(array, mask, count):
    return lax.ppermute(array, AXES, [(i, i ^ mask) for i in range(count)])


def local(velocity, rate, forcing, anchor_line, anchor_z, assign, spectral, dense, momentum):
    n_grp, n_slab = lax.axis_size("grp"), lax.axis_size("slab")
    devices = n_grp * n_slab
    width = dense.shape[1]
    lines = anchor_line.shape[0]
    cells_x, _, cells_z = velocity.shape
    chunks = cells_z // LANES
    halo_rows = LAYERS * 8 * chunks
    piece = momentum.shape[0]
    packed = piece // 2
    f32 = jnp.float32
    joined = n_grp == 2 and piece == width and devices & (devices - 1) == 0
    two_sided = n_grp != 2
    table, wave_table = (jnp.asarray(array) for array in tables())
    spectral, dense = spectral.T, dense.T

    sides = 2 if two_sided else 1
    edge_rows = halo_rows + (packed if joined else 0)
    message = ((halo_rows, LANES), f32)
    corner_message = ((-(-chunks // 8) * 8, LANES), f32)
    velocity, rate, forcing, near_momentum, dense, table, wave_table, to_a, to_b, *edges = call(
        functools.partial(edge_kernel, joined, sides),
        [(velocity.shape, f32)] * 3
        + [(array.shape, array.dtype) for array in (momentum, dense, table, wave_table)]
        + [message, message]
        + [((edge_rows, LANES), f32)] * sides + [corner_message] * sides,
        scratch=[pltpu.SemaphoreType.DMA((7,))],
        ins=[HBM] * 7,
    )(*(in_hbm(array) for array in (velocity, rate, forcing, momentum, dense, table, wave_table)))
    far = far_map(n_grp, n_slab)
    near = {i: i ^ 1 for i in range(devices)}
    if two_sided:
        moves = [{i: i + n_slab for i in range(devices - n_slab)}, {i: i - n_slab for i in range(n_slab, devices)}]
        inner = [i for i in range(devices) if 0 < i % n_slab < n_slab - 1]
        diagonal_far = [{i: far[move[i]] for i in inner if i in move} for move in moves]
    else:
        moves = [{i: i ^ n_slab for i in range(devices)}]
        ends = (0, n_slab - 1)
        diagonal_far = [{i: i ^ n_slab if i % n_slab in ends else far[i ^ n_slab] for i in range(devices)}]
    from_grp = [hop(array, move) for array, move in zip(edges, moves)]
    from_b = hop(to_b, far)
    corners = [hop(array, move) for array, move in zip(edges[sides:], diagonal_far)]
    rows = halo_rows + -(-sides * chunks // 8) * 8
    to_a = call(
        functools.partial(near_kernel, sides, chunks), [((rows, LANES), f32)], ins=[VMEM] * (1 + sides)
    )(to_a, *from_grp)[0]
    from_a = hop(to_a, near)
    pay_rows = -(-(MODES + 2 + n_grp) // 8) * 8
    scale = 1.0 / (devices * lines * SUB)
    window = ((8 * cells_x, cells_z + LANES), f32)
    previous, change, payload = call(
        functools.partial(step_kernel, two_sided, width, scale),
        [window, window, ((pay_rows, LANES), f32)],
        scratch=[pltpu.SMEM((lines,), jnp.int32)] * 3 + [
            pltpu.SemaphoreType.DMA((3,)),
            pltpu.VMEM((lines, SUB), f32),
            pltpu.VMEM((2, LANES, 2 * SUB), jnp.bfloat16),
            pltpu.VMEM((2, 2 * width, 2 * SUB), jnp.bfloat16),
        ],
        ins=[VMEM] * (5 + 2 * sides) + [HBM] * 3 + [VMEM] * 4,
    )(velocity, rate, forcing, *from_grp, from_a, from_b, *corners,
      in_hbm(anchor_line), in_hbm(anchor_z), in_hbm(assign.reshape(-1)), spectral, dense, table, wave_table)

    masks = hop_masks(n_grp, n_slab)
    if joined:
        mine = jnp.concatenate([edges[0][halo_rows:], from_grp[0][halo_rows:]], axis=0)
        order = [n_slab] + masks[3:] + masks[2:3] + [1]
        for mask in order[1:-1]:
            other = swap(mine, mask, devices)
            mine = jnp.concatenate([mine, other], axis=0)
        other = swap(mine, order[-1], devices)
        base = call(
            functools.partial(base_kernel, order[:-1], width), [(spectral.shape, f32)], ins=[VMEM] * 3
        )(spectral, mine, other)[0]
    else:
        whole = lax.all_gather(momentum, AXES, axis=0, tiled=True)
        base = spectral - (learn_rate * decay_rate) * whole.T
    anchor = payload
    if devices & (devices - 1) == 0:
        for number, mask in enumerate(masks):
            payload = payload + swap(payload, mask, devices)
            if number == 0:
                anchor = payload
    else:
        payload = lax.psum(payload, AXES)
    field_now = call(field_kernel, [(velocity.shape, f32)], ins=[VMEM, VMEM, HBM])(previous, change, anchor)[0]
    rows, spread, turned = call(
        functools.partial(prepare_kernel, width),
        [((8, LANES), f32), ((LANES, 2 * MODES * width), jnp.bfloat16), (((MODES + 1) * width, LANES), f32)],
        ins=[VMEM] * 2,
    )(spectral, dense)
    groups = 4
    spectral_new, dense_new, momentum_new, trainer_loss = call(
        functools.partial(update_kernel, width, lines, groups),
        [(spectral.shape, f32), (dense.shape, f32), (momentum.shape, f32), ((1, 1), f32)],
        scratch=[
            pltpu.VMEM((LANES, LANES), f32), pltpu.VMEM(spectral.shape, f32), pltpu.VMEM(dense.shape, f32),
            pltpu.VMEM(momentum.shape, f32), pltpu.VMEM((1, 1), f32), pltpu.SemaphoreType.DMA((groups + 3,)),
        ],
        ins=[VMEM] * 7,
        places=[HBM] * 4,
    )(payload, base, dense, near_momentum, rows, spread, turned)
    return (field_now, trainer_loss, spectral_new.T, dense_new.T, momentum_new)


def solution(mesh):
    placed = (
        P("grp", "slab", None),
        P("grp", "slab", None),
        P("grp", "slab", None),
        P(("grp", "slab")),
        P(("grp", "slab")),
        P(("grp", "slab"), None),
        P(),
        P(),
        P(("grp", "slab"), None),
    )

    return jax.shard_map(
        local,
        mesh=mesh,
        in_specs=placed,
        out_specs=(P("grp", "slab", None), P("grp", "slab"), P(), P(), P(("grp", "slab"), None)),
        check_vma=False,
    )
```

```python
import functools
import math

import jax
import jax.numpy as jnp
import numpy as np
from jax import lax
from jax.experimental import pallas as pl
from jax.experimental.pallas import tpu as pltpu
from jax.sharding import PartitionSpec as P


SUB = 128
MODES = 16
LANES = 128
FEATURES = 2 * MODES + 8

decay_rate = 0.9
learn_rate = 0.5
dense_rate = 3.0

AXES = ("grp", "slab")
NT = (((1,), (1,)), ((), ()))
VMEM = pl.BlockSpec(memory_space=pltpu.VMEM)
HBM = pl.BlockSpec(memory_space=pltpu.HBM)


def call(kernel, outs, scratch=(), ins=(), places=None, flops=1000000):
    outs = [jax.ShapeDtypeStruct(shape, dtype) for shape, dtype in outs]
    size = sum(math.prod(o.shape) * o.dtype.itemsize for o in outs)
    return pl.pallas_call(
        kernel,
        out_shape=outs,
        in_specs=list(ins),
        out_specs=places or [VMEM] * len(outs),
        scratch_shapes=list(scratch),
        compiler_params=pltpu.CompilerParams(vmem_limit_bytes=16 << 20),
        cost_estimate=pl.CostEstimate(flops=flops, bytes_accessed=2 * size, transcendentals=0),
    )


def halves(array):
    coarse = array.astype(jnp.bfloat16).astype(jnp.float32)
    return coarse, array - coarse


def tables():
    counts = np.arange(SUB)
    waves = np.arange(MODES)
    angle = (waves[:, None] * counts[None, :] % SUB) * (2.0 * np.pi / SUB)
    weight = np.where(waves == 0, 1.0, 2.0)[:, None] / SUB
    plain = np.concatenate([np.cos(angle), np.sin(angle)]).astype(np.float32)
    parts = []
    rest = plain
    for _ in range(3):
        parts.append(rest.astype(jnp.bfloat16))
        rest = rest - parts[-1].astype(np.float32)
    high, middle, low = parts
    weighted = np.concatenate([weight * np.cos(angle), weight * np.sin(angle)]).astype(np.float32)
    return weighted, np.concatenate([high, high, middle, middle, high, low], axis=1)


def put_plane(ref, row, plane):
    for q in range(plane.shape[1] // LANES):
        ref[row + 8 * q : row + 8 * q + 8, :] = plane[:, q * LANES : (q + 1) * LANES]


def get_plane(ref, row, chunks):
    return jnp.concatenate([ref[row + 8 * q : row + 8 * q + 8, :] for q in range(chunks)], axis=1)


def put_line(ref, row, line):
    for q in range(line.shape[1] // LANES):
        ref[row + q : row + q + 1, :] = line[:, q * LANES : (q + 1) * LANES]


def get_line(ref, row, chunks):
    return jnp.concatenate([ref[row + q : row + q + 1, :] for q in range(chunks)], axis=1)


def pack_rows(block):
    half = block.shape[0] // 2
    return jnp.concatenate([block[:half], block[half:]], axis=1)


LAYERS = 3


def beside_in_z(plane):
    size = plane.shape[1]
    return pltpu.roll(plane, 1, 1) + pltpu.roll(plane, size - 1, 1)


def shifted(plane, before, after):
    sublane = lax.broadcasted_iota(jnp.int32, plane.shape, 0)
    last = plane.shape[0] - 1
    up = jnp.where(sublane == last, after, pltpu.roll(plane, last, 0))
    down = jnp.where(sublane == 0, before, pltpu.roll(plane, 1, 0))
    return up, down


def edge_kernel(
    with_momentum, sides, v_hbm, rate_hbm, forcing_hbm, momentum_hbm, dense_hbm, table_hbm, wave_hbm, *rest
):
    v_ref, rate_ref, forcing_ref, momentum_ref, dense_ref, table_ref, wave_ref, a_ref, b_ref = rest[:9]
    rest = rest[3:]
    across = rest[6 : 6 + sides]
    corners = rest[6 + sides : 6 + 2 * sides]
    sems = rest[-1]
    pairs = (
        (momentum_hbm, momentum_ref), (v_hbm, v_ref), (rate_hbm, rate_ref), (forcing_hbm, forcing_ref),
        (dense_hbm, dense_ref), (table_hbm, table_ref), (wave_hbm, wave_ref),
    )
    moves = [pltpu.make_async_copy(*pair, sems.at[number]) for number, pair in enumerate(pairs)]
    for move in moves:
        move.start()
    last = v_ref.shape[0] - 1
    chunks = v_ref.shape[2] // LANES
    even = lax.rem(lax.axis_index("slab"), 2) == 0
    moves[0].wait()
    if with_momentum:
        packed = pack_rows(momentum_ref[...].T)
        start = LAYERS * 8 * chunks
        across[0][start : start + packed.shape[0], :] = packed
    for move in moves[1:]:
        move.wait()

    def message(edge, inside, rate, forcing):
        up, down = shifted(edge, 0.0, 0.0)
        partial = edge + (rate * (inside + up + down + beside_in_z(edge) - 6.0 * edge) + forcing)
        return edge, rate, partial

    highs = [lax.axis_index("grp") == 0] if sides == 1 else [True, False]
    for number, high in enumerate(highs):
        edge, inside = jnp.where(high, last, 0), jnp.where(high, last - 1, 1)
        planes = message(v_ref[edge], v_ref[inside], rate_ref[edge], forcing_ref[edge])
        for layer, plane in enumerate(planes):
            put_plane(across[number], layer * 8 * chunks, plane)
        left, right = planes[0][0:1], planes[0][planes[0].shape[0] - 1 :]
        corners[number][...] = jnp.zeros_like(corners[number])
        put_line(corners[number], 0, jnp.where(even, left, right))
    last = v_ref.shape[1] - 1
    lefts, rights = (
        message(v_ref[:, at, :], v_ref[:, inside, :], rate_ref[:, at, :], forcing_ref[:, at, :])
        for at, inside in ((0, 1), (last, last - 1))
    )
    for layer, (left, right) in enumerate(zip(lefts, rights)):
        put_plane(a_ref, layer * 8 * chunks, jnp.where(even, right, left))
        put_plane(b_ref, layer * 8 * chunks, jnp.where(even, left, right))


def grp_halo(two_sided, refs, layer, chunks):
    rows = 8 * chunks * layer
    if two_sided:
        return get_plane(refs[0], rows, chunks), get_plane(refs[1], rows, chunks)
    plane = get_plane(refs[0], rows, chunks)
    first = lax.axis_index("grp") == 0
    return jnp.where(first, 0.0, plane), jnp.where(first, plane, 0.0)


def near_kernel(sides, chunks, message_ref, *refs):
    across, out_ref = refs[:sides], refs[sides]
    even = lax.rem(lax.axis_index("slab"), 2) == 0
    rows = message_ref.shape[0]
    out_ref[0:rows, :] = message_ref[...]
    out_ref[rows:, :] = jnp.zeros((out_ref.shape[0] - rows, LANES), jnp.float32)
    for number in range(sides):
        plane = get_plane(across[number], 0, chunks)
        last = plane.shape[0] - 1
        put_line(out_ref, rows + number * chunks, jnp.where(even, plane[last:], plane[0:1]))


def as_row(column):
    size = column.shape[0]
    square = (size, size)
    same = lax.broadcasted_iota(jnp.int32, square, 0) == lax.broadcasted_iota(jnp.int32, square, 1)
    return jnp.sum(jnp.where(same, column, 0.0), axis=0, keepdims=True)


def feature_map(width, spectral_ref, dense_ref):
    gain = as_row(dense_ref[:, width : width + 1])
    bias = as_row(dense_ref[:, width + 1 : width + 2])
    gains = jnp.concatenate([gain, gain], axis=1)
    lane = lax.broadcasted_iota(jnp.int32, (width, LANES), 1)
    low = lane < width
    full = jnp.zeros((width, LANES), jnp.float32)
    for pair in range(MODES):
        product = spectral_ref[:, pair * LANES : (pair + 1) * LANES] * gains
        first = jnp.sum(jnp.where(low, product, 0.0), axis=1, keepdims=True)
        second = jnp.sum(jnp.where(low, 0.0, product), axis=1, keepdims=True)
        full = jnp.where(lane == 2 * pair, first, jnp.where(lane == 2 * pair + 1, second, full))
    mixing = dense_ref[:, 0:width]
    by_input = jnp.sum(gain * mixing, axis=1, keepdims=True)
    by_one = jnp.sum(bias * (mixing + spectral_ref[:, 0:width]), axis=1, keepdims=True)
    by_one = by_one + dense_ref[:, width + 2 : width + 3]
    full = jnp.where(lane == 2 * MODES, by_input, jnp.where(lane == 2 * MODES + 1, by_one, full))
    coarse, fine = halves(full)
    joined = coarse + pltpu.roll(coarse, FEATURES, 1) + pltpu.roll(fine, 2 * FEATURES, 1)
    return joined.astype(jnp.bfloat16)


def step_kernel(two_sided, width, scale, v_ref, rate_ref, forcing_ref, *refs):
    sides = 2 if two_sided else 1
    across, (a_ref, b_ref) = refs[:sides], refs[sides : sides + 2]
    corners, refs = refs[sides + 2 : 2 * sides + 2], refs[2 * sides + 2 :]
    line_hbm, start_hbm, assign_hbm, spectral_ref, dense_ref, table_ref, wave_ref = refs[:7]
    previous, change, pay_ref, line_ref, start_ref, assign_ref, sems = refs[7:14]
    inputs_ref, feature_ref, slope_ref = refs[14:]
    moves = [
        pltpu.make_async_copy(source, target, sems.at[number])
        for number, (source, target) in enumerate(
            ((line_hbm, line_ref), (start_hbm, start_ref), (assign_hbm, assign_ref))
        )
    ]
    for move in moves:
        move.start()
    cells_x, cells_y, cells_z = v_ref.shape
    chunks = cells_z // LANES
    slab = lax.axis_index("slab")
    even = lax.rem(slab, 2) == 0
    inner = jnp.logical_and(slab > 0, slab < lax.axis_size("slab") - 1)

    def slab_layer(layer):
        from_a = get_plane(a_ref, 8 * chunks * layer, chunks)
        from_b = jnp.where(inner, get_plane(b_ref, 8 * chunks * layer, chunks), 0.0)
        return jnp.where(even, from_b, from_a), jnp.where(even, from_a, from_b)

    def corner(side):
        here = True if two_sided else lax.axis_index("grp") == 1 - side

        number = side if two_sided else 0
        from_a = get_line(a_ref, LAYERS * 8 * chunks + number * chunks, chunks)
        from_b = get_line(corners[number], 0, chunks)
        from_a = jnp.where(here, from_a, 0.0)
        from_b = jnp.where(jnp.logical_and(here, inner), from_b, 0.0)
        return jnp.where(even, from_b, from_a), jnp.where(even, from_a, from_b)

    def tendency(plane, above, below, up, down, rate, forcing):
        beside = above + below + up + down + beside_in_z(plane)
        return rate * (beside - 6.0 * plane) + forcing

    low, high = grp_halo(two_sided, across, 0, chunks)
    low_rate, high_rate = grp_halo(two_sided, across, 1, chunks)
    low_part, high_part = grp_halo(two_sided, across, 2, chunks)
    left, right = slab_layer(0)
    left_rate, right_rate = slab_layer(1)
    left_part, right_part = slab_layer(2)
    sublane = lax.broadcasted_iota(jnp.int32, (cells_y, cells_z), 0)

    def halo_step(part, rate, inner_plane, ends):
        last = part.shape[0] - 1
        at_ends = jnp.where(sublane == 0, ends[0], jnp.where(sublane == last, ends[1], 0.0))
        return part + rate * (inner_plane + at_ends)

    low_left, low_right = corner(0)
    high_left, high_right = corner(1)
    planes = [low] + [v_ref[i] for i in range(cells_x)] + [high]
    stepped = [halo_step(low_part, low_rate, planes[1], (low_left, low_right))]
    for i in range(cells_x):
        plane = planes[i + 1]
        up, down = shifted(plane, left[i : i + 1], right[i : i + 1])
        stepped.append(plane + tendency(plane, planes[i + 2], planes[i], up, down, rate_ref[i], forcing_ref[i]))
    stepped.append(halo_step(high_part, high_rate, planes[cells_x], (high_left, high_right)))
    left_new = halo_step(left_part, left_rate, v_ref[:, 0, :], (low_left, high_left))
    right_new = halo_step(right_part, right_rate, v_ref[:, cells_y - 1, :], (low_right, high_right))
    for i in range(cells_x):
        plane = stepped[i + 1]
        up, down = shifted(plane, left_new[i : i + 1], right_new[i : i + 1])
        moved = tendency(plane, stepped[i + 2], stepped[i], up, down, rate_ref[i], forcing_ref[i])
        previous[8 * i : 8 * i + 8, 0:cells_z] = plane
        change[8 * i : 8 * i + 8, 0:cells_z] = moved
    count = line_ref.shape[0]
    previous[:, cells_z : cells_z + LANES] = jnp.zeros((8 * cells_x, LANES), jnp.float32)
    change[:, cells_z : cells_z + LANES] = jnp.zeros((8 * cells_x, LANES), jnp.float32)
    channel_map = feature_map(width, spectral_ref, dense_ref)
    for move in moves:
        move.wait()

    def window(ref, t):
        line, start = line_ref[t], start_ref[t]
        inside = start & (LANES - 1)
        base = pl.multiple_of(start - inside, LANES)
        row = ref[pl.ds(line, 1), pl.ds(base, 2 * LANES)]
        return pltpu.roll(row, (2 * LANES - inside) & (2 * LANES - 1), 1)[:, :SUB]

    targets = []
    for t in range(count):
        inputs_ref[t : t + 1, :] = window(previous, t)
        targets.append(window(change, t))

    cos_w, sin_w = table_ref[0:MODES, :], table_ref[MODES:, :]
    coarse, rest = halves(inputs_ref[...])
    middle, fine = halves(rest)
    parts = jnp.concatenate([coarse, middle, coarse, middle, fine, coarse], axis=1).astype(jnp.bfloat16)
    waves = lax.dot_general(wave_ref[...], parts, NT, preferred_element_type=jnp.float32)
    tail = lax.broadcasted_iota(jnp.int32, (8, SUB), 0)
    half_projection = jnp.broadcast_to(0.5 * dense_ref[:, width + 3 : width + 4], (width, SUB))
    held = jnp.zeros((width, SUB), jnp.float32)
    lane = lax.broadcasted_iota(jnp.int32, (1, LANES), 1)
    losses = jnp.zeros((1, LANES), jnp.float32)
    root = math.sqrt(2.0 / math.pi)
    bend = 0.044715
    group = 2
    pairs = None
    for t in range(count):
        real, imag = waves[:MODES, t : t + 1], waves[MODES:, t : t + 1]
        line = inputs_ref[t : t + 1, :]
        rest = jnp.where(tail == 0, line, jnp.where(tail == 1, 1.0, 0.0))
        feature = jnp.concatenate([real * cos_w + imag * sin_w, imag * cos_w - real * sin_w, rest], axis=0)
        coarse, fine = halves(feature)
        zeros = jnp.zeros((LANES - 3 * FEATURES, SUB), jnp.float32)
        stack = jnp.concatenate([coarse, fine, coarse, zeros], axis=0).astype(jnp.bfloat16)
        at = slice(t % group * SUB, (t % group + 1) * SUB)
        feature_ref[t // group % 2, :, at] = stack
        before = jnp.dot(channel_map, stack, preferred_element_type=jnp.float32)
        square = before * before
        grown = 1.0 + jnp.tanh(before * (root + (root * bend) * square))
        after = before * grown
        slope = grown * (1.0 + (2.0 - grown) * (before * (root + (3.0 * root * bend) * square)))
        output = jnp.sum(after * half_projection, axis=0, keepdims=True)
        differ = output - targets[t]
        error = jnp.sum(differ * differ, axis=1, keepdims=True)
        losses = losses + jnp.where(lane == assign_ref[t], error, 0.0)
        pull = (2.0 * scale) * differ
        held = held + after * pull
        coarse, fine = halves(slope * (half_projection * pull))
        slope_ref[t // group % 2, 0:width, at] = coarse.astype(jnp.bfloat16)
        slope_ref[t // group % 2, width : 2 * width, at] = fine.astype(jnp.bfloat16)
        if (t + 1) % group == 0 or t + 1 == count:
            span = slice(0, (t % group + 1) * SUB)
            part = lax.dot_general(
                feature_ref[t // group % 2, :, span], slope_ref[t // group % 2, :, span], NT,
                preferred_element_type=jnp.float32,
            )[0 : 2 * FEATURES]
            pairs = part if pairs is None else pairs + part
    total = pairs[0:FEATURES, 0:width] + pairs[FEATURES : 2 * FEATURES, 0:width] + pairs[0:FEATURES, width:]
    pay_ref[...] = jnp.zeros_like(pay_ref)
    pay_ref[0:MODES, :] = jnp.concatenate([total[0:MODES], total[MODES : 2 * MODES]], axis=1)
    row = 2 * MODES
    pay_ref[MODES : MODES + 1, :] = jnp.concatenate([total[row : row + 1], total[row + 1 : row + 2]], axis=1)
    pay_ref[MODES + 1 : MODES + 2, 0:width] = as_row(0.5 * jnp.sum(held, axis=1, keepdims=True))
    pay_ref[pl.ds(MODES + 2 + lax.axis_index("grp"), 1), :] = losses


def field_kernel(previous, change, _, out_ref):
    cells_x, _, cells_z = out_ref.shape
    for i in range(cells_x):
        at = slice(8 * i, 8 * i + 8)
        out_ref[i] = previous[at, 0:cells_z] + change[at, 0:cells_z]


def base_kernel(masks, width, spectral_ref, mine_ref, other_ref, out_ref):
    here = lax.axis_index("grp") * lax.axis_size("slab") + lax.axis_index("slab")
    rows = width // 2
    low = lax.broadcasted_iota(jnp.int32, (rows, LANES), 1) < width
    even = lax.rem(here, 2) == 0
    for number in range(mine_ref.shape[0] // rows):
        source = here
        twin_even = twin_odd = 0
        for bit, (at_even, at_odd) in enumerate(masks):
            if number >> bit & 1:
                source = source ^ jnp.where(even, at_even, at_odd)
                twin_even |= 1 << [odd for _, odd in masks].index(at_even)
                twin_odd |= 1 << [ev for ev, _ in masks].index(at_odd)
        twin = jnp.where(even, twin_even, twin_odd)
        columns = pl.ds(pl.multiple_of((source // 2) * LANES, LANES), LANES)
        mine = mine_ref[number * rows : (number + 1) * rows, :]
        other = other_ref[pl.ds(pl.multiple_of(twin * rows, rows), rows), :]
        first, second = jnp.where(even, mine, other), jnp.where(even, other, mine)
        top = jnp.where(low, first, pltpu.roll(second, width, 1))
        bottom = jnp.where(low, pltpu.roll(first, width, 1), second)
        factor = learn_rate * decay_rate
        out_ref[0:rows, columns] = spectral_ref[0:rows, columns] - factor * top
        out_ref[rows : 2 * rows, columns] = spectral_ref[rows : 2 * rows, columns] - factor * bottom


def prepare_kernel(width, spectral_ref, dense_ref, row_ref, spread_ref, turned_ref):
    row_ref[...] = jnp.zeros_like(row_ref)
    for number in range(2):
        row = as_row(dense_ref[:, width + number : width + number + 1])
        row_ref[number : number + 1, :] = jnp.concatenate([row, row], axis=1)
    tall = 2 * 8
    lane = lax.broadcasted_iota(jnp.int32, (tall, LANES), 1)
    row = lax.broadcasted_iota(jnp.int32, (tall, LANES), 0)
    low = lane < width
    gain, gain_rest = halves(learn_rate * row_ref[0:1, :])
    bias, bias_rest = halves(learn_rate * row_ref[1:2, :])
    parts = ((gain, bias), (gain_rest, bias_rest), (gain, bias))
    half = MODES // 2
    for pair in range(MODES):
        first = 2 * pair if pair < half else 2 * pair + 2
        for group in range(LANES // tall):
            block = jnp.zeros((tall, LANES), jnp.float32)
            for part, (gains, biases) in enumerate(parts):
                at = part * FEATURES + first - group * tall
                if -1 <= at < tall:
                    block = jnp.where(row == jnp.where(low, at, at + 1), gains, block)
                at = part * FEATURES + 2 * MODES + 2 - group * tall
                if pair == 0 and 0 <= at < tall:
                    block = jnp.where(jnp.logical_and(row == at, low), biases, block)
            columns = slice(pair * LANES, (pair + 1) * LANES)
            spread_ref[group * tall : (group + 1) * tall, columns] = block.astype(jnp.bfloat16)
    for pair in range(half):
        real = spectral_ref[:, pair * LANES : (pair + 1) * LANES].T
        imag = spectral_ref[:, (half + pair) * LANES : (half + pair + 1) * LANES].T
        turned_ref[pair * LANES : (pair + 1) * LANES, :] = jnp.concatenate([real, imag], axis=1)
    mixing = dense_ref[:, 0:width]
    both = jnp.concatenate([mixing, mixing + spectral_ref[:, 0:width]], axis=1).T
    turned_ref[MODES * width :, :] = jnp.concatenate([both[0:width], both[width:]], axis=1)


def update_kernel(
    width, lines, groups, pay_ref, base_ref, dense_ref, momentum_ref, row_ref, spread_ref, turned_ref,
    spectral_hbm, dense_hbm, momentum_hbm, loss_hbm, square, result, dense_out, momentum_out, loss_out, sems,
):
    first, second = lax.axis_index("grp"), lax.axis_index("slab")
    here = first * lax.axis_size("slab") + second
    copies = []

    def send(source, target):
        copies.append(pltpu.make_async_copy(source, target, sems.at[len(copies)]))
        copies[-1].start()

    kept = pay_ref.shape[0]
    square[0:kept, :] = pay_ref[...]
    square[kept:, :] = jnp.zeros((LANES - kept, LANES), jnp.float32)
    turned = square[...].T
    lane = lax.broadcasted_iota(jnp.int32, (width, LANES), 1)
    real, imag = turned[0:width], turned[width : 2 * width]
    factors = jnp.where(lane < MODES + 2, real, 0.0) + pltpu.roll(jnp.where(lane <= MODES, imag, 0.0), MODES + 2, 1)
    coarse, fine = halves(factors)
    stack = coarse + pltpu.roll(coarse, FEATURES, 1) + pltpu.roll(fine, 2 * FEATURES, 1)
    stack = stack.astype(jnp.bfloat16)
    columns = 2 * MODES * width // groups
    for group in range(groups):
        span = slice(group * columns, (group + 1) * columns)
        gradient = jnp.dot(stack, spread_ref[:, span], preferred_element_type=jnp.float32)
        result[:, span] = base_ref[:, span] - gradient
        send(result.at[:, pl.ds(group * columns, columns)], spectral_hbm.at[:, pl.ds(group * columns, columns)])

    slopes = pay_ref[MODES : MODES + 1, :]
    gain, bias = dense_ref[:, width : width + 1], dense_ref[:, width + 1 : width + 2]
    piece = momentum_ref.shape[0]
    block = here * piece // width
    inside = here * piece - block * width
    square[0:width, :] = jnp.where(lane < width, gain, bias)
    at = pl.ds(0 if piece == width else pl.multiple_of(inside, piece), piece)
    half = block // MODES
    row = pay_ref[pl.ds(block - half * MODES, 1), :]
    row = jnp.where(half == 0, row[:, 0:width], row[:, width:])
    gradient = square[at, 0:width] * row
    gradient = gradient + jnp.where(block == 0, square[at, width : 2 * width] * slopes[:, width:], 0.0)
    momentum_out[...] = decay_rate * momentum_ref[...] + gradient
    send(momentum_out, momentum_hbm)
    sums = pay_ref[pl.ds(MODES + 2 + first, 1), :]
    lane1 = lax.broadcasted_iota(jnp.int32, (1, LANES), 1)
    own = jnp.sum(jnp.where(lane1 == second, sums, 0.0), axis=1, keepdims=True)
    loss_out[...] = own * (1.0 / (lines * SUB))
    send(loss_out, loss_hbm)

    last = turned_ref[MODES * width :, :] * slopes
    gathered = jnp.where(lane < width, last, 0.0)
    for mode in range(MODES):
        gathered = gathered + turned_ref[mode * width : (mode + 1) * width, :] * pay_ref[mode : mode + 1, :]
    by_gain = jnp.sum(gathered, axis=1, keepdims=True)
    by_bias = jnp.sum(jnp.where(lane < width, 0.0, last), axis=1, keepdims=True)
    by_input, by_output, by_one = real[:, MODES : MODES + 1], real[:, MODES + 1 : MODES + 2], imag[:, MODES : MODES + 1]
    mixing = row_ref[0:1, 0:width] * by_input + row_ref[1:2, 0:width] * by_one
    dense_out[:, 0:width] = dense_ref[:, 0:width] - dense_rate * mixing
    lane4 = lax.broadcasted_iota(jnp.int32, (width, 4), 1)
    change = jnp.where(
        lane4 == 0, by_gain, jnp.where(lane4 == 1, by_bias, jnp.where(lane4 == 2, by_one, by_output)))
    dense_out[:, width : width + 4] = dense_ref[:, width : width + 4] - dense_rate * change
    send(dense_out, dense_hbm)
    for copy in copies:
        copy.wait()


def hop_masks(n_grp, n_slab):
    slab_bits = [1 << bit for bit in range(n_slab.bit_length() - 1)]
    grp_bits = [n_slab << bit for bit in range(n_grp.bit_length() - 1)]
    return [1] + [mask + 1 for mask in grp_bits + slab_bits[1:2] + slab_bits[:1:-1]]


def far_map(n_grp, n_slab):
    targets = {}
    for i in range(n_grp * n_slab):
        grp, slab = i // n_slab, i % n_slab
        if 0 < slab < n_slab - 1:
            targets[i] = i + 1 if slab % 2 else i - 1
        elif n_grp % 2 == 0:
            targets[i] = (grp ^ 1) * n_slab + slab
    return targets


def hop(array, targets):
    return lax.ppermute(array, AXES, sorted(targets.items()))


def in_hbm(array):
    return pltpu.with_memory_space_constraint(array, pltpu.HBM)


def swap(array, mask, count):
    return lax.ppermute(array, AXES, [(i, i ^ mask) for i in range(count)])


def local(velocity, rate, forcing, anchor_line, anchor_z, assign, spectral, dense, momentum):
    n_grp, n_slab = lax.axis_size("grp"), lax.axis_size("slab")
    devices = n_grp * n_slab
    width = dense.shape[1]
    lines = anchor_line.shape[0]
    cells_x, _, cells_z = velocity.shape
    chunks = cells_z // LANES
    halo_rows = LAYERS * 8 * chunks
    piece = momentum.shape[0]
    packed = piece // 2
    f32 = jnp.float32
    joined = n_grp == 2 and piece == width and devices & (devices - 1) == 0
    two_sided = n_grp != 2
    table, wave_table = (jnp.asarray(array) for array in tables())
    spectral, dense = spectral.T, dense.T

    sides = 2 if two_sided else 1
    edge_rows = halo_rows + (packed if joined else 0)
    message = ((halo_rows, LANES), f32)
    corner_message = ((-(-chunks // 8) * 8, LANES), f32)
    velocity, rate, forcing, near_momentum, dense, table, wave_table, to_a, to_b, *edges = call(
        functools.partial(edge_kernel, joined, sides),
        [(velocity.shape, f32)] * 3
        + [(array.shape, array.dtype) for array in (momentum, dense, table, wave_table)]
        + [message, message]
        + [((edge_rows, LANES), f32)] * sides + [corner_message] * sides,
        scratch=[pltpu.SemaphoreType.DMA((7,))],
        ins=[HBM] * 7,
    )(*(in_hbm(array) for array in (velocity, rate, forcing, momentum, dense, table, wave_table)))
    far = far_map(n_grp, n_slab)
    near = {i: i ^ 1 for i in range(devices)}
    if two_sided:
        moves = [{i: i + n_slab for i in range(devices - n_slab)}, {i: i - n_slab for i in range(n_slab, devices)}]
        inner = [i for i in range(devices) if 0 < i % n_slab < n_slab - 1]
        diagonal_far = [{i: far[move[i]] for i in inner if i in move} for move in moves]
    else:
        moves = [{i: i ^ n_slab for i in range(devices)}]
        ends = (0, n_slab - 1)
        diagonal_far = [{i: i ^ n_slab if i % n_slab in ends else far[i ^ n_slab] for i in range(devices)}]
    from_grp = [hop(array, move) for array, move in zip(edges, moves)]
    from_b = hop(to_b, far)
    corners = [hop(array, move) for array, move in zip(edges[sides:], diagonal_far)]
    rows = halo_rows + -(-sides * chunks // 8) * 8
    to_a = call(
        functools.partial(near_kernel, sides, chunks), [((rows, LANES), f32)], ins=[VMEM] * (1 + sides)
    )(to_a, *from_grp)[0]
    from_a = hop(to_a, near)
    pay_rows = -(-(MODES + 2 + n_grp) // 8) * 8
    scale = 1.0 / (devices * lines * SUB)
    window = ((8 * cells_x, cells_z + LANES), f32)
    previous, change, payload = call(
        functools.partial(step_kernel, two_sided, width, scale),
        [window, window, ((pay_rows, LANES), f32)],
        scratch=[pltpu.SMEM((lines,), jnp.int32)] * 3 + [
            pltpu.SemaphoreType.DMA((3,)),
            pltpu.VMEM((lines, SUB), f32),
            pltpu.VMEM((2, LANES, 2 * SUB), jnp.bfloat16),
            pltpu.VMEM((2, 2 * width, 2 * SUB), jnp.bfloat16),
        ],
        ins=[VMEM] * (5 + 2 * sides) + [HBM] * 3 + [VMEM] * 4,
    )(velocity, rate, forcing, *from_grp, from_a, from_b, *corners,
      in_hbm(anchor_line), in_hbm(anchor_z), in_hbm(assign.reshape(-1)), spectral, dense, table, wave_table)

    masks = hop_masks(n_grp, n_slab)
    if joined:
        mine = jnp.concatenate([edges[0][halo_rows:], from_grp[0][halo_rows:]], axis=0)
        bits = [1 << bit for bit in range(n_slab.bit_length() - 2, 0, -1)]
        order = list(zip(bits, bits[:-2] + bits[-2:][::-1]))
        for at_even, at_odd in order:
            other = hop(mine, {i: i ^ (at_odd if i & 1 else at_even) for i in range(devices)})
            mine = jnp.concatenate([mine, other], axis=0)
        other = hop(mine, near)
        order = [(n_slab, n_slab)] + order
        base = call(
            functools.partial(base_kernel, order, width), [(spectral.shape, f32)], ins=[VMEM] * 3
        )(spectral, mine, other)[0]
    else:
        whole = lax.all_gather(momentum, AXES, axis=0, tiled=True)
        base = spectral - (learn_rate * decay_rate) * whole.T
    anchor = payload
    if devices & (devices - 1) == 0:
        for number, mask in enumerate(masks):
            payload = payload + swap(payload, mask, devices)
            if number == 0:
                anchor = payload
    else:
        payload = lax.psum(payload, AXES)
    field_now = call(field_kernel, [(velocity.shape, f32)], ins=[VMEM, VMEM, HBM])(previous, change, anchor)[0]
    rows, spread, turned = call(
        functools.partial(prepare_kernel, width),
        [((8, LANES), f32), ((LANES, 2 * MODES * width), jnp.bfloat16), (((MODES + 1) * width, LANES), f32)],
        ins=[VMEM] * 2,
    )(spectral, dense)
    groups = 4
    spectral_new, dense_new, momentum_new, trainer_loss = call(
        functools.partial(update_kernel, width, lines, groups),
        [(spectral.shape, f32), (dense.shape, f32), (momentum.shape, f32), ((1, 1), f32)],
        scratch=[
            pltpu.VMEM((LANES, LANES), f32), pltpu.VMEM(spectral.shape, f32), pltpu.VMEM(dense.shape, f32),
            pltpu.VMEM(momentum.shape, f32), pltpu.VMEM((1, 1), f32), pltpu.SemaphoreType.DMA((groups + 3,)),
        ],
        ins=[VMEM] * 7,
        places=[HBM] * 4,
    )(payload, base, dense, near_momentum, rows, spread, turned)
    return (field_now, trainer_loss, spectral_new.T, dense_new.T, momentum_new)


def solution(mesh):
    placed = (
        P("grp", "slab", None),
        P("grp", "slab", None),
        P("grp", "slab", None),
        P(("grp", "slab")),
        P(("grp", "slab")),
        P(("grp", "slab"), None),
        P(),
        P(),
        P(("grp", "slab"), None),
    )

    return jax.shard_map(
        local,
        mesh=mesh,
        in_specs=placed,
        out_specs=(P("grp", "slab", None), P("grp", "slab"), P(), P(), P(("grp", "slab"), None)),
        check_vma=False,
    )
```
